128 devices in a mesh: row: 16 (over x, y_hi, core), col: 8 (over z, y_lo).
Axes of the slice: x: 4, y: 4 (y_hi: 2, y_lo: 2; y = y_hi * 2 + y_lo), z: 4, core: 2. Of those that a mesh axis runs over, the one named last changes fastest.
Arguments:
- a_vals: bfloat16 [512, 8, 64, 1024], P('row', 'col'), may hold values from -0.0625 to 0.0625
- a_cols: int32 [512, 8, 16], P('row', 'col'), may hold values from 0 to 63, all different within a row
- p_vals: bfloat16 [512, 64, 256], P(('row', 'col')), may hold values from -1.5 to 1.5
- p_cols: int32 [512, 4], P(('row', 'col')), may hold values from 0 to 15, all different within a row
Outputs:
- coarse_op: float32 [1024, 1024], P('row', 'col')
The draws below stay inside these ranges and needn't reach their ends.
Inputs may be any that keep to these rules, and one draw needn't show every extreme that they name: `a_cols`: within one fine block row and column range the 16 entries are distinct. `p_cols`: within one fine block row the 4 entries are distinct.
All inputs are finite; a program needn't handle non-finite values.
Results may differ from the reference program's by a relative error of at most 0.0003.
Values may be sent and summed in bfloat16 or wider, within the bound.
No kernel may reach another device: no remote copies, remote signals or barrier semaphores. Data moves between devices by JAX's collectives and lax.ppermute only.
A program may use at most 128 MiB of HBM per device.

```python
import jax
import jax.numpy as jnp
from jax import lax

BS = 64
KA = 16
KP = 4
NF = 512
FC = 64
NC = 16
N_COL = 8


def block_levels(rng, shape, split, low, largest):
    level = 1.0
    for axis_at, shards_of in split:
        steps = jax.random.uniform(jax.random.fold_in(jax.random.fold_in(rng, 6), axis_at), (shards_of,), jnp.float32, low / len(split), largest / len(split))
        level = level * jnp.repeat(jnp.exp(steps), shape[axis_at] // shards_of).reshape((-1,) + (1,) * (len(shape) - 1 - axis_at))
    return level


def distinct(rng, rows, count, top, lift):
    sequence = jax.random.permutation(jax.random.fold_in(rng, 1), count)
    favour = sequence
    for power in range(3):
        favour = favour * favour // count
    favour = favour * lift // count
    chance = jax.random.randint(jax.random.fold_in(rng, 2), (rows, count), 0, 4096) + favour
    sure = jax.random.permutation(jax.random.fold_in(rng, 3), rows)[jnp.arange(count) % rows]
    chance = jnp.where(jnp.arange(rows)[:, None] == sure[None, :], 1 << 14, chance)
    score = chance * count + jnp.arange(count)
    return lax.top_k(score.astype(jnp.int32), top)[1].astype(jnp.int32)


def noise(stream_key, extent, spread, bound, split=(), kind=jnp.bfloat16):
    level = block_levels(stream_key, extent, split, -0.22, 0.18) if split else 1.0
    values = jax.random.normal(stream_key, extent, jnp.float32) * spread * level
    return jnp.minimum(jnp.maximum(values, -bound), bound).astype(kind)


def setup_inputs(seed: int = 0) -> dict:
    key_list = jax.random.split(jax.random.key(seed), 5)
    return {
        "a_vals": noise(key_list[0], (NF, N_COL, BS, KA * BS), (N_COL * KA * BS) ** -0.5, 0.0625, ((0, 16), (1, 8))),
        "a_cols": distinct(key_list[1], NF * N_COL, FC, KA, 0).reshape((NF, N_COL, KA)),
        "p_vals": noise(key_list[2], (NF, BS, KP * BS), 0.25, 1.5, ((0, 128),)),
        "p_cols": distinct(key_list[3], NF, NC, KP, 0),
    }


def densify(vals, ids):
    count = vals.shape[0]
    onehot = (ids[:, :, None] == jnp.arange(NC, dtype=jnp.int32)[None, None, :]).astype(jnp.float32)
    tiles = vals.reshape(count, BS, KP, BS).astype(jnp.float32)
    dense = jnp.einsum("nrkd,nkq->nrqd", tiles, onehot)
    return dense.astype(jnp.bfloat16).reshape(count, BS, NC * BS)


def reference(a_vals, a_cols, p_vals, p_cols):
    dense_p = densify(p_vals, p_cols)
    offsets = (jnp.arange(N_COL, dtype=jnp.int32) * FC)[None, :, None]
    global_cols = (a_cols + offsets).astype(jnp.int32)
    group = 2

    def step(total, index):
        start = (index * group).astype(jnp.int32)
        rows_a = lax.dynamic_slice_in_dim(a_vals, start, group, 0)
        rows_c = lax.dynamic_slice_in_dim(global_cols, start, group, 0)
        rows_p = lax.dynamic_slice_in_dim(dense_p, start, group, 0)
        picked = dense_p[rows_c.reshape(-1)].reshape(group, N_COL * KA * BS, NC * BS)
        left = jnp.transpose(rows_a, (0, 2, 1, 3)).reshape(group, BS, N_COL * KA * BS)
        product = jnp.einsum("irf,ifq->irq", left.astype(jnp.float32), picked.astype(jnp.float32))
        flat_p = rows_p.reshape(group * BS, NC * BS).astype(jnp.float32)
        flat_w = product.reshape(group * BS, NC * BS)
        total = total + jnp.dot(flat_p.T, flat_w, precision=lax.Precision.HIGHEST)
        return total, None

    start_total = jnp.zeros((NC * BS, NC * BS), jnp.float32)
    total, unused = lax.scan(step, start_total, jnp.arange(NF // group, dtype=jnp.int32))
    return total
```

```python
import functools

import jax
import jax.numpy as jnp
from jax import lax
from jax.experimental import pallas as pl
from jax.experimental.pallas import tpu as pltpu
from jax.sharding import Mesh
from jax.sharding import PartitionSpec as P

AXES = ("x", "yh", "core", "z", "yl")
SIZES = (4, 2, 2, 4, 2)
BF16 = jnp.bfloat16
F32 = jnp.float32
BS = 64
PAD = 16


def linear(place):
    index = 0
    for at, size in zip(place, SIZES):
        index = index * size + at
    return index


def route(target):
    pairs = []
    for x in range(4):
        for yh in range(2):
            for core in range(2):
                for z in range(4):
                    for yl in range(2):
                        to_x, to_y, to_core, to_z = target(x, 2 * yh + yl, core, z)
                        to_x, to_y, to_z = to_x % 4, to_y % 4, to_z % 4
                        to = linear((to_x, to_y // 2, to_core, to_z, to_y % 2))
                        pairs.append((linear((x, yh, core, z, yl)), to))
    return pairs


def swap_y(y):
    return (y % 2) * 2 + y // 2


MIRROR = route(lambda x, y, c, z: (z, swap_y(y), c, x))
MIRROR_FAR = route(lambda x, y, c, z: (z, swap_y(y) + 2, c, x))
OTHER_CORE = route(lambda x, y, c, z: (x, y, 1 - c, z))
NEXT_X = route(lambda x, y, c, z: (x + 1, y, c, z))
LAST_X = route(lambda x, y, c, z: (x - 1, y, c, z))
NEXT_Z = route(lambda x, y, c, z: (x, y, c, z + 1))
LAST_Z = route(lambda x, y, c, z: (x, y, c, z - 1))
BESIDE = route(lambda x, y, c, z: (x, y ^ 1, c, z))


def send(value, pairs):
    return lax.ppermute(value, AXES, pairs)


def ring_of_four(own, forward, backward):
    half = own.shape[0] // 2
    behind = send(own, forward)
    ahead = send(own, backward)
    far_a = send(behind[:half], forward)
    far_b = send(ahead[half:], backward)
    return own, behind, ahead, far_a, far_b


def spread(tile, ids, coarse_pairs, store):
    lane = lax.broadcasted_iota(jnp.int32, (1, 128), 1)
    low = lane < BS
    parts = []
    for pair in range(2):
        v = tile[:, 128 * pair : 128 * (pair + 1)]
        r = jnp.concatenate([v[:, BS:], v[:, :BS]], axis=1)
        d = ids[:, 128 * pair : 128 * (pair + 1)]
        e = jnp.concatenate([d[:, BS:], d[:, :BS]], axis=1)
        parts.append((jnp.where(low, v, r), jnp.where(low, d, e)))
        parts.append((jnp.where(low, r, v), jnp.where(low, e, d)))
    for g in range(coarse_pairs):
        here = jnp.where(low, 2.0 * g, 2.0 * g + 1.0)
        out = jnp.zeros((BS, 128), tile.dtype)
        for v, d in parts:
            out = jnp.where(jnp.broadcast_to(d == here, (BS, 128)), v, out)
        store(g, out)


def galerkin(cols_ref, core_ref, a_ref, pc_ref, pr_ref, own_ref, other_ref, dense, turned, hi, lo):
    core = core_ref[0]
    pieces = pc_ref.shape[0]
    fine_rows = a_ref.shape[0]

    @pl.loop(0, pieces)
    def _(piece):
        for b in range(4):
            tile = pc_ref[piece, pl.ds(BS * b, BS), :].astype(F32)
            ids = pc_ref[piece, pl.ds(4 * BS, PAD), :].astype(F32)[b : b + 1]

            def store(g, out):
                dense[4 * piece + b, :, 128 * g : 128 * (g + 1)] = out.astype(BF16)

            spread(tile, ids, 8, store)

    @pl.loop(0, pr_ref.shape[0])
    def _(piece):
        ids4 = pr_ref[piece, pl.ds(4 * BS, PAD), :].astype(F32)
        lane = lax.broadcasted_iota(jnp.int32, (1, 128), 1)
        low = lane < BS
        for pair in range(2):
            tile = pr_ref[piece, pl.ds(128 * pair, 128), :].astype(F32)
            flipped = tile.T
            ida = ids4[2 * pair : 2 * pair + 1]
            idb = ids4[2 * pair + 1 : 2 * pair + 2]
            where = []
            for m in range(4):
                a = ida[:, BS * m : BS * (m + 1)]
                b = idb[:, BS * m : BS * (m + 1)]
                where.append(jnp.concatenate([a, b], axis=1))
            for n in range(16):
                out = jnp.zeros((BS, 128), F32)
                for m in range(4):
                    hit = jnp.broadcast_to(where[m] == float(n), (BS, 128))
                    out = jnp.where(hit, flipped[BS * m : BS * (m + 1)], out)
                slot = core if n % 2 == 0 else 1 - core
                at = pl.multiple_of(256 * piece + 128 * pair, 128)
                turned[slot, pl.ds(BS * (n // 2), BS), pl.ds(at, 128)] = out.astype(BF16)

    @pl.loop(0, fine_rows)
    def _(i):
        for n in range(4):
            total = None
            for k in range(4):
                tiles = [
                    dense[cols_ref[i, 4 * k + j], :, 256 * n : 256 * (n + 1)] for j in range(4)
                ]
                weights = jnp.concatenate(tiles, axis=0)
                left = a_ref[i, :, 256 * k : 256 * (k + 1)]
                part = jnp.dot(left, weights, preferred_element_type=F32)
                total = part if total is None else total + part
            top = total.astype(BF16)
            rows = pl.ds(pl.multiple_of(i * BS, BS), BS)
            hi[rows, 256 * n : 256 * (n + 1)] = top
            lo[rows, 256 * n : 256 * (n + 1)] = (total - top.astype(F32)).astype(BF16)

    for slot, out_ref in ((1, other_ref), (0, own_ref)):

        @pl.loop(0, 4)
        def _(n):
            at = pl.ds(pl.multiple_of(256 * n, 256), 256)
            left = turned[slot]
            c = jnp.dot(left, hi[:, at], preferred_element_type=F32)
            c = c + jnp.dot(left, lo[:, at], preferred_element_type=F32)
            for q in range(8):
                for j in range(2):
                    out_ref[8 * q + 2 * n + j] = c[
                        BS * q : BS * (q + 1), 128 * j : 128 * (j + 1)
                    ]


def compute(cols, core, a, pc, pr):
    half = jax.ShapeDtypeStruct((64, BS, 128), F32)
    vmem = pl.BlockSpec(memory_space=pltpu.VMEM)
    smem = pl.BlockSpec(memory_space=pltpu.SMEM)
    rows = a.shape[0] * BS
    return pl.pallas_call(
        galerkin,
        out_shape=(half, half),
        in_specs=[smem, smem, vmem, vmem, vmem],
        out_specs=(vmem, vmem),
        scratch_shapes=[
            pltpu.VMEM((64, BS, 1024), BF16),
            pltpu.VMEM((2, 512, rows), BF16),
            pltpu.VMEM((rows, 1024), BF16),
            pltpu.VMEM((rows, 1024), BF16),
        ],
        compiler_params=pltpu.CompilerParams(vmem_limit_bytes=48 << 20),
        name="galerkin",
    )(cols, core, a, pc, pr)


def gather_pieces(piece):
    near = send(piece, MIRROR)
    far = send(piece, MIRROR_FAR)
    yh = lax.axis_index("yh")
    x = lax.axis_index("x")
    z = lax.axis_index("z")
    yl = lax.axis_index("yl")
    rows = piece.shape[0]
    pair = jnp.stack([jnp.where(yh == 0, near, far), jnp.where(yh == 0, far, near)])
    own, behind, ahead, far_a, far_b = ring_of_four(pair, NEXT_X, LAST_X)
    opposite = jnp.concatenate([far_a, far_b])
    ring = jnp.stack([own, ahead, opposite, behind])
    ring = jnp.roll(ring, x, axis=0)
    half = ring.reshape(8, rows, piece.shape[1])
    other = send(half, OTHER_CORE)
    core = lax.axis_index("core")
    pc = jnp.concatenate([jnp.where(core == 0, half, other), jnp.where(core == 0, other, half)])

    beside = send(piece, BESIDE)
    pair = jnp.stack([jnp.where(yl == 0, piece, beside), jnp.where(yl == 0, beside, piece)])
    own, behind, ahead, far_a, far_b = ring_of_four(pair, NEXT_Z, LAST_Z)
    opposite = jnp.concatenate([far_a, far_b])
    ring = jnp.stack([own, ahead, opposite, behind])
    ring = jnp.roll(ring, z, axis=0)
    pr = ring.reshape(8, rows, piece.shape[1])
    return pc, pr


def shards(a_vals, a_cols, p_vals, p_cols):
    ids = jnp.repeat(p_cols.astype(BF16), BS, axis=1)
    piece = jnp.concatenate([p_vals.reshape(4 * BS, 4 * BS), ids, jnp.zeros((PAD - 4, 4 * BS), BF16)])
    pc, pr = gather_pieces(piece)
    core = lax.axis_index("core").astype(jnp.int32).reshape(1)
    own, other = compute(a_cols[:, 0], core, a_vals[:, 0], pc, pr)
    total = own + send(other, OTHER_CORE)
    mixed = lax.all_to_all(total, ("x", "yh", "z", "yl"), 0, 0, tiled=True)
    return jnp.sum(mixed, axis=0)


def solution(mesh):
    fine = Mesh(mesh.devices.reshape(SIZES), AXES)
    row, col = ("x", "yh", "core"), ("z", "yl")
    in_specs = (
        P(row, col, None, None),
        P(row, col, None),
        P(row + col, None, None),
        P(row + col, None),
    )
    return jax.shard_map(
        shards, mesh=fine, in_specs=in_specs, out_specs=P(row, col), check_vma=False
    )
```

```python
import jax
import jax.numpy as jnp
from jax import lax
from jax.experimental import pallas as pl
from jax.experimental.pallas import tpu as pltpu
from jax.sharding import Mesh
from jax.sharding import PartitionSpec as P

AXES = ("x", "yh", "core", "z", "yl")
SIZES = (4, 2, 2, 4, 2)
BF16 = jnp.bfloat16
F32 = jnp.float32
BS = 64
ROWS = 72
PAD = 16


def linear(place):
    index = 0
    for at, size in zip(place, SIZES):
        index = index * size + at
    return index


def route(target):
    pairs = []
    for x in range(4):
        for yh in range(2):
            for core in range(2):
                for z in range(4):
                    for yl in range(2):
                        to_x, to_y, to_core, to_z = target(x, 2 * yh + yl, core, z)
                        to_x, to_y, to_z = to_x % 4, to_y % 4, to_z % 4
                        to = linear((to_x, to_y // 2, to_core, to_z, to_y % 2))
                        pairs.append((linear((x, yh, core, z, yl)), to))
    return pairs


def swap_y(y):
    return (y % 2) * 2 + y // 2


REFLECT = route(lambda x, y, c, z: (2 * x - z, swap_y(y), c, x))
REFLECT_FAR = route(lambda x, y, c, z: (2 * x - z, swap_y(y) + 2, c, x))
OTHER_CORE = route(lambda x, y, c, z: (x, y, 1 - c, z))
NEXT_X = route(lambda x, y, c, z: (x + 1, y, c, z))
LAST_X = route(lambda x, y, c, z: (x - 1, y, c, z))
NEXT_Z = route(lambda x, y, c, z: (x, y, c, z + 1))
LAST_Z = route(lambda x, y, c, z: (x, y, c, z - 1))
BESIDE = route(lambda x, y, c, z: (x, y ^ 1, c, z))


def send(value, pairs):
    return lax.ppermute(value, AXES, pairs)


def together(*values):
    return lax.optimization_barrier(values)


def spread(tile, ids, coarse_pairs, store):
    lane = lax.broadcasted_iota(jnp.int32, (1, 128), 1)
    low = lane < BS
    parts = []
    for pair in range(2):
        v = tile[:, 128 * pair : 128 * (pair + 1)]
        r = jnp.concatenate([v[:, BS:], v[:, :BS]], axis=1)
        d = ids[:, 128 * pair : 128 * (pair + 1)]
        e = jnp.concatenate([d[:, BS:], d[:, :BS]], axis=1)
        parts.append((jnp.where(low, v, r), jnp.where(low, d, e)))
        parts.append((jnp.where(low, r, v), jnp.where(low, e, d)))
    for g in range(coarse_pairs):
        here = jnp.where(low, 2.0 * g, 2.0 * g + 1.0)
        out = jnp.zeros((BS, 128), tile.dtype)
        for v, d in parts:
            out = jnp.where(jnp.broadcast_to(d == here, (BS, 128)), v, out)
        store(g, out)


def galerkin(cols_ref, core_ref, slot_c, slot_r, a_hbm, *refs):
    pc_in, pr_in, refs = refs[:10], refs[10:15], refs[15:]
    own_ref, other_ref, a_ref, pc_ref, pr_ref, dense, turned, hi, lo, sems = refs
    core = core_ref[0]
    pieces = pc_ref.shape[0]
    fine_rows = a_ref.shape[0]
    copies = []
    for group, held in ((pc_in, pc_ref), (pr_in, pr_ref)):
        at = 0
        for ref in group:
            here = held.at[pl.ds(at, ref.shape[0])]
            copies.append(pltpu.make_async_copy(ref, here, sems.at[len(copies)]))
            at += ref.shape[0]
    copies.append(pltpu.make_async_copy(a_hbm, a_ref, sems.at[len(copies)]))
    for copy in copies:
        copy.start()
    for copy in copies[:10]:
        copy.wait()

    @pl.loop(0, pieces)
    def _(piece):
        for b in range(4):
            tile = pc_ref[piece, pl.ds(BS * b, BS), :].astype(F32)
            ids = pc_ref[piece, pl.ds(4 * BS, PAD), :].astype(F32)[b : b + 1]

            def store(g, out):
                dense[4 * slot_c[piece] + b, :, 128 * g : 128 * (g + 1)] = out.astype(BF16)

            spread(tile, ids, 8, store)

    for copy in copies[10:15]:
        copy.wait()

    @pl.loop(0, pr_ref.shape[0])
    def _(piece):
        ids4 = pr_ref[piece, pl.ds(4 * BS, PAD), :].astype(F32)
        lane = lax.broadcasted_iota(jnp.int32, (1, 128), 1)
        low = lane < BS
        for pair in range(2):
            tile = pr_ref[piece, pl.ds(128 * pair, 128), :].astype(F32)
            flipped = tile.T
            ida = ids4[2 * pair : 2 * pair + 1]
            idb = ids4[2 * pair + 1 : 2 * pair + 2]
            where = []
            for m in range(4):
                a = ida[:, BS * m : BS * (m + 1)]
                b = idb[:, BS * m : BS * (m + 1)]
                where.append(jnp.concatenate([a, b], axis=1))
            for n in range(16):
                out = jnp.zeros((BS, 128), F32)
                for m in range(4):
                    hit = jnp.broadcast_to(where[m] == float(n), (BS, 128))
                    out = jnp.where(hit, flipped[BS * m : BS * (m + 1)], out)
                slot = core if n % 2 == 0 else 1 - core
                at = pl.multiple_of(256 * slot_r[piece] + 128 * pair, 128)
                turned[slot, pl.ds(BS * (n // 2), BS), pl.ds(at, 128)] = out.astype(BF16)

    copies[15].wait()

    @pl.loop(0, fine_rows)
    def _(i):
        for n in range(4):
            total = None
            for k in range(4):
                tiles = [
                    dense[cols_ref[i, 4 * k + j], :, 256 * n : 256 * (n + 1)] for j in range(4)
                ]
                weights = jnp.concatenate(tiles, axis=0)
                left = a_ref[i, :, 256 * k : 256 * (k + 1)]
                part = jnp.dot(left, weights, preferred_element_type=F32)
                total = part if total is None else total + part
            top = total.astype(BF16)
            rows = pl.ds(pl.multiple_of(i * BS, BS), BS)
            hi[rows, 256 * n : 256 * (n + 1)] = top
            lo[rows, 256 * n : 256 * (n + 1)] = (total - top.astype(F32)).astype(BF16)

    for slot, out_ref in ((1, other_ref), (0, own_ref)):

        @pl.loop(0, 4)
        def _(n):
            at = pl.ds(pl.multiple_of(256 * n, 256), 256)
            left = turned[slot]
            c = jnp.dot(left, hi[:, at], preferred_element_type=F32)
            c = c + jnp.dot(left, lo[:, at], preferred_element_type=F32)
            for q in range(8):
                for j in range(2):
                    out_ref[8 * q + 2 * n + j] = c[
                        BS * q : BS * (q + 1), 128 * j : 128 * (j + 1)
                    ]


def compute(cols, core, slot_c, slot_r, a, pc, pr):
    half = jax.ShapeDtypeStruct((64, BS, 128), F32)
    vmem = pl.BlockSpec(memory_space=pltpu.VMEM)
    smem = pl.BlockSpec(memory_space=pltpu.SMEM)
    hbm = pl.BlockSpec(memory_space=pl.ANY)
    rows = a.shape[0] * BS
    piece = pc[0].shape[1:]
    return pl.pallas_call(
        galerkin,
        out_shape=(half, half),
        in_specs=[smem] * 4 + [hbm] * 16,
        out_specs=(vmem, vmem),
        scratch_shapes=[
            pltpu.VMEM(a.shape, BF16),
            pltpu.VMEM((16,) + piece, BF16),
            pltpu.VMEM((8,) + piece, BF16),
            pltpu.VMEM((64, BS, 1024), BF16),
            pltpu.VMEM((2, 512, rows), BF16),
            pltpu.VMEM((rows, 1024), BF16),
            pltpu.VMEM((rows, 1024), BF16),
            pltpu.SemaphoreType.DMA((16,)),
        ],
        compiler_params=pltpu.CompilerParams(vmem_limit_bytes=48 << 20),
        name="galerkin",
    )(cols, core, slot_c, slot_r, a, *pc, *pr)


def gather_pieces(piece):
    near, far, beside = together(
        send(piece, REFLECT), send(piece, REFLECT_FAR), send(piece, BESIDE)
    )
    c0 = jnp.concatenate([near, far])
    r0 = jnp.concatenate([piece, beside])
    c1, c2, r1, r2, d0 = together(
        send(c0, NEXT_X), send(c0, LAST_X), send(r0, NEXT_Z), send(r0, LAST_Z), send(c0, OTHER_CORE)
    )
    c3, c4, r3, r4, d1, d2 = together(
        send(c1[:1], NEXT_X),
        send(c2[1:], LAST_X),
        send(r1[:1], NEXT_Z),
        send(r2[1:], LAST_Z),
        send(c1, OTHER_CORE),
        send(c2, OTHER_CORE),
    )
    d3, d4 = send(c3, OTHER_CORE), send(c4, OTHER_CORE)
    return (c0, c1, c2, c3, c4, d0, d1, d2, d3, d4), (r0, r1, r2, r3, r4)


def slots():
    x, yh, core, z, yl = (lax.axis_index(name).astype(jnp.int32) for name in AXES)
    step = jnp.array([0, 0, -1, -1, 1, 1, 2, 2], jnp.int32)
    side = jnp.array([0, 1, 0, 1, 0, 1, 0, 1], jnp.int32)
    mine = 2 * ((2 * z - x - step) % 4) + (yh ^ side)
    slot_c = jnp.concatenate([mine + 8 * core, mine + 8 * (1 - core)])
    slot_r = 2 * ((z + step) % 4) + (yl ^ side)
    return core.reshape(1), slot_c, slot_r


def pack(a_ref, b_ref, out_ref):
    total = a_ref[...] + b_ref[...]
    largest = jnp.max(jnp.abs(total), axis=1, keepdims=True)
    power = jnp.clip(jnp.ceil(jnp.log2(jnp.maximum(largest, 1e-36))), -110.0, 60.0)
    scaled = total * jnp.exp2(15.0 - power)
    scaled = jnp.clip(jnp.floor(scaled + 0.5), -32767.0, 32767.0)
    out_ref[:, :BS, :] = scaled.astype(jnp.int32).astype(jnp.int16)
    power = jnp.broadcast_to(power, (power.shape[0], ROWS - BS, 128))
    out_ref[:, BS:, :] = power.astype(jnp.int32).astype(jnp.int16)


def unpack(in_ref, out_ref):
    def step(j, total):
        value = in_ref[j].astype(jnp.int32).astype(F32)
        return total + value[:BS] * jnp.exp2(value[BS : BS + 1] - 15.0)

    out_ref[...] = lax.fori_loop(0, in_ref.shape[0], step, jnp.zeros((BS, 128), F32), unroll=4)


def packed_sum(a, b):
    block = pl.BlockSpec((8, BS, 128), lambda i: (i, 0, 0))
    return pl.pallas_call(
        pack,
        grid=(8,),
        out_shape=jax.ShapeDtypeStruct((64, ROWS, 128), jnp.int16),
        in_specs=[block, block],
        out_specs=pl.BlockSpec((8, ROWS, 128), lambda i: (i, 0, 0)),
        name="pack",
    )(a, b)


def unpacked_sum(mixed):
    return pl.pallas_call(
        unpack, out_shape=jax.ShapeDtypeStruct((BS, 128), F32), name="unpack"
    )(mixed)


def shards(a_vals, a_cols, p_vals, p_cols):
    ids = jnp.repeat(p_cols.astype(BF16), BS, axis=1)
    blank = jnp.zeros((PAD - 4, 4 * BS), BF16)
    piece = jnp.concatenate([p_vals.reshape(4 * BS, 4 * BS), ids, blank])
    pc, pr = gather_pieces(piece[None])
    core, slot_c, slot_r = slots()
    own, other = compute(a_cols[:, 0], core, slot_c, slot_r, a_vals[:, 0], pc, pr)
    packed = packed_sum(own, send(other, OTHER_CORE))
    mixed = lax.all_to_all(packed, ("x", "yh", "z", "yl"), 0, 0, tiled=True)
    return unpacked_sum(mixed)


def solution(mesh):
    fine = Mesh(mesh.devices.reshape(SIZES), AXES)
    row, col = ("x", "yh", "core"), ("z", "yl")
    in_specs = (
        P(row, col, None, None),
        P(row, col, None),
        P(row + col, None, None),
        P(row + col, None),
    )
    return jax.shard_map(
        shards, mesh=fine, in_specs=in_specs, out_specs=P(row, col), check_vma=False
    )
```

```python
import jax
import jax.numpy as jnp
from jax import lax
from jax.experimental import pallas as pl
from jax.experimental.pallas import tpu as pltpu
from jax.sharding import Mesh
from jax.sharding import PartitionSpec as P

AXES = ("x", "yh", "core", "z", "yl")
SIZES = (4, 2, 2, 4, 2)
BF16 = jnp.bfloat16
F32 = jnp.float32
BS = 64
ROWS = 72
PAD = 16


def linear(place):
    index = 0
    for at, size in zip(place, SIZES):
        index = index * size + at
    return index


def route(target):
    pairs = []
    for x in range(4):
        for yh in range(2):
            for core in range(2):
                for z in range(4):
                    for yl in range(2):
                        to_x, to_y, to_core, to_z = target(x, 2 * yh + yl, core, z)
                        to_x, to_y, to_z = to_x % 4, to_y % 4, to_z % 4
                        to = linear((to_x, to_y // 2, to_core, to_z, to_y % 2))
                        pairs.append((linear((x, yh, core, z, yl)), to))
    return pairs


def swap_y(y):
    return (y % 2) * 2 + y // 2


REFLECT = route(lambda x, y, c, z: (2 * x - z, swap_y(y), c, x))
REFLECT_FAR = route(lambda x, y, c, z: (2 * x - z, swap_y(y) + 2, c, x))
OTHER_CORE = route(lambda x, y, c, z: (x, y, 1 - c, z))
NEXT_X = route(lambda x, y, c, z: (x + 1, y, c, z))
LAST_X = route(lambda x, y, c, z: (x - 1, y, c, z))
NEXT_Z = route(lambda x, y, c, z: (x, y, c, z + 1))
LAST_Z = route(lambda x, y, c, z: (x, y, c, z - 1))
ACROSS_Z = route(lambda x, y, c, z: (x, y, c, z + 2))
BESIDE = route(lambda x, y, c, z: (x, y ^ 1, c, z))


def send(value, pairs):
    return lax.ppermute(value, AXES, pairs)


def together(*values):
    return lax.optimization_barrier(values)


def rows16(row):
    return jnp.broadcast_to(row.astype(F32), (16, 128)).astype(BF16)


def choose(ids, number, values):
    out = [jnp.zeros((16, 128), BF16)] * 4
    for value, at in zip(values, ids):
        hit = at == number
        out = [jnp.where(hit, value[16 * t : 16 * (t + 1)], out[t]) for t in range(4)]
    return jnp.concatenate(out, axis=0)


def swap_halves(v):
    return jnp.concatenate([v[:, BS:], v[:, :BS]], axis=1)


def spread(tile, ids, store):
    low = lax.broadcasted_iota(jnp.int32, (BS, 128), 1) < BS
    low1 = lax.broadcasted_iota(jnp.int32, (1, 128), 1) < BS
    values, where = [], []
    for pair in range(2):
        v = tile[:, 128 * pair : 128 * (pair + 1)].astype(F32)
        r = swap_halves(v)
        d = ids[:, 128 * pair : 128 * (pair + 1)]
        e = swap_halves(d)
        values += [jnp.where(low, v, r).astype(BF16), jnp.where(low, r, v).astype(BF16)]
        for full in (jnp.where(low1, d, e), jnp.where(low1, e, d)):
            where.append(rows16(full - jnp.where(low1, 0.0, 1.0)))
    for g in range(8):
        store(g, choose(where, jnp.asarray(2.0 * g, BF16), values))


def fine_product(cols_ref, slot_c, a_hbm, *refs):
    pc_in, (hi, lo, a_ref, pc_ref, dense, sems) = refs[:10], refs[10:]
    copies, at = [], 0
    for ref in pc_in:
        here = pc_ref.at[pl.ds(at, ref.shape[0])]
        copies.append(pltpu.make_async_copy(ref, here, sems.at[len(copies)]))
        at += ref.shape[0]
    fetch = pltpu.make_async_copy(a_hbm, a_ref, sems.at[10])
    fetch.start()
    for copy in copies:
        copy.start()
    for copy in copies:
        copy.wait()

    @pl.loop(0, pc_ref.shape[0])
    def _(piece):
        ids = pc_ref[piece, pl.ds(4 * BS, PAD), :].astype(F32)
        for b in range(4):

            def store(g, out):
                dense[4 * slot_c[piece] + b, :, 128 * g : 128 * (g + 1)] = out

            spread(pc_ref[piece, pl.ds(BS * b, BS), :], ids[b : b + 1], store)

    fetch.wait()

    @pl.loop(0, a_ref.shape[0])
    def _(i):
        for n in range(4):
            total = None
            for k in range(4):
                tiles = [
                    dense[cols_ref[i, 4 * k + j], :, 256 * n : 256 * (n + 1)] for j in range(4)
                ]
                weights = jnp.concatenate(tiles, axis=0)
                left = a_ref[i, :, 256 * k : 256 * (k + 1)]
                part = jnp.dot(left, weights, preferred_element_type=F32)
                total = part if total is None else total + part
            top = total.astype(BF16)
            rows = pl.ds(pl.multiple_of(i * BS, BS), BS)
            hi[rows, 256 * n : 256 * (n + 1)] = top
            lo[rows, 256 * n : 256 * (n + 1)] = (total - top.astype(F32)).astype(BF16)


def turn(pr_ref, piece, turned, core, at):
    ids4 = pr_ref[piece, pl.ds(4 * BS, PAD), :].astype(F32)
    for pair in range(2):
        flipped = pr_ref[piece, pl.ds(128 * pair, 128), :].astype(F32).T.astype(BF16)
        where, values = [], []
        for m in range(4):
            a = ids4[2 * pair : 2 * pair + 1, BS * m : BS * (m + 1)]
            b = ids4[2 * pair + 1 : 2 * pair + 2, BS * m : BS * (m + 1)]
            where.append(rows16(jnp.concatenate([a, b], axis=1)))
            values.append(flipped[BS * m : BS * (m + 1)])
        for n in range(16):
            out = choose(where, jnp.asarray(float(n), BF16), values)
            slot = core if n % 2 == 0 else 1 - core
            to = pl.ds(pl.multiple_of(at + 128 * pair, 128), 128)
            turned[slot, pl.ds(BS * (n // 2), BS), to] = out


def half_product(turned, slot, hi, lo, out_ref):
    @pl.loop(0, 4)
    def _(n):
        at = pl.ds(pl.multiple_of(256 * n, 256), 256)
        left = turned[slot]
        c = jnp.dot(left, hi[:, at], preferred_element_type=F32)
        c = c + jnp.dot(left, lo[:, at], preferred_element_type=F32)
        for q in range(8):
            for j in range(2):
                out_ref[8 * q + 2 * n + j] = c[BS * q : BS * (q + 1), 128 * j : 128 * (j + 1)]


def other_half(core_ref, slot_r, hi, lo, r0, r1, r2, r3, turned, out_ref):
    at = 0
    for ref in (r0, r1, r2, r3):

        @pl.loop(0, 2)
        def _(side):
            turn(ref, side, turned, core_ref[0], 256 * slot_r[at + side])

        at += 2
    half_product(turned, 1, hi, lo, out_ref)


def own_half(hi, lo, turned, out_ref):
    half_product(turned, 0, hi, lo, out_ref)


VMEM = pl.BlockSpec(memory_space=pltpu.VMEM)
SMEM = pl.BlockSpec(memory_space=pltpu.SMEM)
ANY = pl.BlockSpec(memory_space=pl.ANY)
HALF = jax.ShapeDtypeStruct((64, BS, 128), F32)


def cost(flops):
    return pl.CostEstimate(flops=flops, bytes_accessed=1 << 23, transcendentals=0)


def run_fine_product(cols, slot_c, a, pc):
    rows = a.shape[0] * BS
    return pl.pallas_call(
        fine_product,
        out_shape=(pltpu.VMEM((rows, 1024), BF16),) * 2,
        in_specs=[SMEM] * 2 + [ANY] * 11,
        out_specs=(VMEM, VMEM),
        scratch_shapes=[
            pltpu.VMEM(a.shape, BF16),
            pltpu.VMEM((16,) + pc[0].shape[1:], BF16),
            pltpu.VMEM((64, BS, 1024), BF16),
            pltpu.SemaphoreType.DMA((11,)),
        ],
        compiler_params=pltpu.CompilerParams(vmem_limit_bytes=28 << 20),
        cost_estimate=cost(2 << 33),
        name="fine_product",
    )(cols, slot_c, a, *pc)


def run_other_half(core, slot_r, hi, lo, pr):
    return pl.pallas_call(
        other_half,
        out_shape=(pltpu.VMEM((2, 512, hi.shape[0]), BF16), HALF),
        in_specs=[SMEM] * 2 + [VMEM] * 6,
        out_specs=(VMEM, VMEM),
        compiler_params=pltpu.CompilerParams(vmem_limit_bytes=28 << 20),
        cost_estimate=cost(1 << 33),
        name="other_half",
    )(core, slot_r, hi, lo, *pr)


def run_own_half(hi, lo, turned):
    return pl.pallas_call(
        own_half,
        out_shape=HALF,
        in_specs=[VMEM] * 3,
        out_specs=VMEM,
        compiler_params=pltpu.CompilerParams(vmem_limit_bytes=28 << 20),
        cost_estimate=cost(1 << 33),
        name="own_half",
    )(hi, lo, turned)


def gather_pieces(piece):
    near, far, beside = together(
        send(piece, REFLECT), send(piece, REFLECT_FAR), send(piece, BESIDE)
    )
    c0 = jnp.concatenate([near, far])
    r0 = jnp.concatenate([piece, beside])
    c1, c2, d0 = together(send(c0, NEXT_X), send(c0, LAST_X), send(c0, OTHER_CORE))
    c3, c4, d1, d2, r0 = together(
        send(c1[:1], NEXT_X), send(c2[1:], LAST_X), send(c1, OTHER_CORE), send(c2, OTHER_CORE), r0
    )
    d3, d4 = send(c3, OTHER_CORE), send(c4, OTHER_CORE)
    r1, r2, r3 = send(r0, NEXT_Z), send(r0, LAST_Z), send(r0, ACROSS_Z)
    return (c0, c1, c2, c3, c4, d0, d1, d2, d3, d4), (r0, r1, r2, r3)


def slots():
    x, yh, core, z, yl = (lax.axis_index(name).astype(jnp.int32) for name in AXES)
    step = jnp.array([0, 0, -1, -1, 1, 1, 2, 2], jnp.int32)
    side = jnp.array([0, 1, 0, 1, 0, 1, 0, 1], jnp.int32)
    mine = 2 * ((2 * z - x - step) % 4) + (yh ^ side)
    slot_c = jnp.concatenate([mine + 8 * core, mine + 8 * (1 - core)])
    slot_r = 2 * ((z + step) % 4) + (yl ^ side)
    return core.reshape(1), slot_c, slot_r


def pack(a_ref, b_ref, out_ref):
    @pl.loop(0, a_ref.shape[0])
    def _(i):
        total = a_ref[i] + b_ref[i]
        largest = jnp.max(jnp.abs(total), axis=0, keepdims=True)
        power = jnp.clip(jnp.ceil(jnp.log2(jnp.maximum(largest, 1e-36))), -110.0, 60.0)
        scaled = jnp.floor(total * jnp.exp2(15.0 - power) + 0.5)
        scaled = jnp.minimum(scaled, 32767.0)
        out_ref[i, :BS, :] = scaled.astype(jnp.int32).astype(jnp.int16)
        power = jnp.broadcast_to(power, (ROWS - BS, 128))
        out_ref[i, BS:, :] = power.astype(jnp.int32).astype(jnp.int16)


def unpack(in_ref, out_ref):
    def step(j, total):
        value = in_ref[j].astype(jnp.int32).astype(F32)
        return total + value[:BS] * jnp.exp2(value[BS : BS + 1] - 15.0)

    out_ref[...] = lax.fori_loop(0, in_ref.shape[0], step, jnp.zeros((BS, 128), F32), unroll=4)


def packed_sum(a, b):
    return pl.pallas_call(
        pack,
        out_shape=jax.ShapeDtypeStruct((64, ROWS, 128), jnp.int16),
        in_specs=[VMEM, VMEM],
        out_specs=VMEM,
        name="pack",
    )(a, b)


def unpacked_sum(mixed):
    return pl.pallas_call(
        unpack, out_shape=jax.ShapeDtypeStruct((BS, 128), F32), name="unpack"
    )(mixed)


def shards(a_vals, a_cols, p_vals, p_cols):
    ids = jnp.repeat(p_cols.astype(BF16), BS, axis=1)
    blank = jnp.zeros((PAD - 4, 4 * BS), BF16)
    piece = jnp.concatenate([p_vals.reshape(4 * BS, 4 * BS), ids, blank])
    pc, pr = gather_pieces(piece[None])
    core, slot_c, slot_r = slots()
    hi, lo = run_fine_product(a_cols[:, 0], slot_c, a_vals[:, 0], pc)
    turned, other = run_other_half(core, slot_r, hi, lo, pr)
    met = send(other, OTHER_CORE)
    own = run_own_half(hi, lo, turned)
    packed = packed_sum(own, met)
    mixed = lax.all_to_all(packed, ("x", "yh", "z", "yl"), 0, 0, tiled=True)
    return unpacked_sum(mixed)


def solution(mesh):
    fine = Mesh(mesh.devices.reshape(SIZES), AXES)
    row, col = ("x", "yh", "core"), ("z", "yl")
    in_specs = (
        P(row, col, None, None),
        P(row, col, None),
        P(row + col, None, None),
        P(row + col, None),
    )
    return jax.shard_map(
        shards, mesh=fine, in_specs=in_specs, out_specs=P(row, col), check_vma=False
    )
```

```python
import jax
import jax.numpy as jnp
from jax import lax
from jax.experimental import pallas as pl
from jax.experimental.pallas import tpu as pltpu
from jax.sharding import Mesh
from jax.sharding import PartitionSpec as P

AXES = ("x", "yh", "core", "z", "yl")
SIZES = (4, 2, 2, 4, 2)
BF16 = jnp.bfloat16
F32 = jnp.float32
BS = 64
ROWS = 72
PAD = 16


def linear(place):
    index = 0
    for at, size in zip(place, SIZES):
        index = index * size + at
    return index


def route(target):
    pairs = []
    for x in range(4):
        for yh in range(2):
            for core in range(2):
                for z in range(4):
                    for yl in range(2):
                        to_x, to_y, to_core, to_z = target(x, 2 * yh + yl, core, z)
                        to_x, to_y, to_z = to_x % 4, to_y % 4, to_z % 4
                        to = linear((to_x, to_y // 2, to_core, to_z, to_y % 2))
                        pairs.append((linear((x, yh, core, z, yl)), to))
    return pairs


def swap_y(y):
    return (y % 2) * 2 + y // 2


REFLECT = route(lambda x, y, c, z: (2 * x - z, swap_y(y), c, x))
REFLECT_FAR = route(lambda x, y, c, z: (2 * x - z, swap_y(y) + 2, c, x))
OTHER_CORE = route(lambda x, y, c, z: (x, y, 1 - c, z))
NEXT_X = route(lambda x, y, c, z: (x + 1, y, c, z))
LAST_X = route(lambda x, y, c, z: (x - 1, y, c, z))
NEXT_Z = route(lambda x, y, c, z: (x, y, c, z + 1))
LAST_Z = route(lambda x, y, c, z: (x, y, c, z - 1))
ACROSS_Z = route(lambda x, y, c, z: (x, y, c, z + 2))
BESIDE = route(lambda x, y, c, z: (x, y ^ 1, c, z))


def send(value, pairs):
    return lax.ppermute(value, AXES, pairs)


def together(*values):
    return lax.optimization_barrier(values)


def rows16(row):
    return jnp.broadcast_to(row.astype(F32), (16, 128)).astype(BF16)


def choose(ids, number, values):
    out = [jnp.zeros((16, 128), BF16)] * 4
    for value, at in zip(values, ids):
        hit = at == number
        out = [jnp.where(hit, value[16 * t : 16 * (t + 1)], out[t]) for t in range(4)]
    return jnp.concatenate(out, axis=0)


def swap_halves(v):
    return jnp.concatenate([v[:, BS:], v[:, :BS]], axis=1)


def spread(tile, ids, store):
    low = lax.broadcasted_iota(jnp.int32, (BS, 128), 1) < BS
    low1 = lax.broadcasted_iota(jnp.int32, (1, 128), 1) < BS
    values, where = [], []
    for pair in range(2):
        v = tile[:, 128 * pair : 128 * (pair + 1)].astype(F32)
        r = swap_halves(v)
        d = ids[:, 128 * pair : 128 * (pair + 1)]
        e = swap_halves(d)
        values += [jnp.where(low, v, r).astype(BF16), jnp.where(low, r, v).astype(BF16)]
        for full in (jnp.where(low1, d, e), jnp.where(low1, e, d)):
            where.append(rows16(full - jnp.where(low1, 0.0, 1.0)))
    for g in range(8):
        store(g, choose(where, jnp.asarray(2.0 * g, BF16), values))


def fine_product(cols_ref, slot_c, a_hbm, *refs):
    pc_in, (hi, lo, a_ref, dense, sem) = refs[:10], refs[10:]
    fetch = pltpu.make_async_copy(a_hbm, a_ref, sem)
    fetch.start()

    def place(ref, piece, at):
        ids = ref[piece, pl.ds(4 * BS, PAD), :].astype(F32)
        for b in range(4):

            def store(g, out):
                dense[4 * slot_c[at] + b, :, 128 * g : 128 * (g + 1)] = out

            spread(ref[piece, pl.ds(BS * b, BS), :], ids[b : b + 1], store)

    at = 0
    for ref in pc_in:
        if ref.shape[0] == 1:
            place(ref, 0, at)
        else:

            @pl.loop(0, ref.shape[0])
            def _(piece):
                place(ref, piece, at + piece)

        at += ref.shape[0]
    fetch.wait()

    @pl.loop(0, a_ref.shape[0])
    def _(i):
        for n in range(4):
            total = None
            for k in range(4):
                tiles = [
                    dense[cols_ref[i, 4 * k + j], :, 256 * n : 256 * (n + 1)] for j in range(4)
                ]
                weights = jnp.concatenate(tiles, axis=0)
                left = a_ref[i, :, 256 * k : 256 * (k + 1)]
                part = jnp.dot(left, weights, preferred_element_type=F32)
                total = part if total is None else total + part
            top = total.astype(BF16)
            rows = pl.ds(pl.multiple_of(i * BS, BS), BS)
            hi[rows, 256 * n : 256 * (n + 1)] = top
            lo[rows, 256 * n : 256 * (n + 1)] = (total - top.astype(F32)).astype(BF16)


def turn(pr_ref, piece, turned, core, at):
    ids4 = pr_ref[piece, pl.ds(4 * BS, PAD), :].astype(F32)
    for pair in range(2):
        flipped = pr_ref[piece, pl.ds(128 * pair, 128), :].astype(F32).T.astype(BF16)
        where, values = [], []
        for m in range(4):
            a = ids4[2 * pair : 2 * pair + 1, BS * m : BS * (m + 1)]
            b = ids4[2 * pair + 1 : 2 * pair + 2, BS * m : BS * (m + 1)]
            where.append(rows16(jnp.concatenate([a, b], axis=1)))
            values.append(flipped[BS * m : BS * (m + 1)])
        for n in range(16):
            out = choose(where, jnp.asarray(float(n), BF16), values)
            slot = core if n % 2 == 0 else 1 - core
            to = pl.ds(pl.multiple_of(at + 128 * pair, 128), 128)
            turned[slot, pl.ds(BS * (n // 2), BS), to] = out


def half_product(turned, slot, hi, lo, out_ref):
    @pl.loop(0, 4)
    def _(n):
        at = pl.ds(pl.multiple_of(256 * n, 256), 256)
        left = turned[slot]
        c = jnp.dot(left, hi[:, at], preferred_element_type=F32)
        c = c + jnp.dot(left, lo[:, at], preferred_element_type=F32)
        for q in range(8):
            for j in range(2):
                out_ref[8 * q + 2 * n + j] = c[BS * q : BS * (q + 1), 128 * j : 128 * (j + 1)]


def other_half(core_ref, slot_r, hi, lo, r0, r1, r2, r3, turned, out_ref):
    at = 0
    for ref in (r0, r1, r2, r3):

        @pl.loop(0, 2)
        def _(side):
            turn(ref, side, turned, core_ref[0], 256 * slot_r[at + side])

        at += 2
    half_product(turned, 1, hi, lo, out_ref)


def own_half(hi, lo, turned, out_ref):
    half_product(turned, 0, hi, lo, out_ref)


VMEM = pl.BlockSpec(memory_space=pltpu.VMEM)
SMEM = pl.BlockSpec(memory_space=pltpu.SMEM)
HBM = pl.BlockSpec(memory_space=pltpu.HBM)
HALF = jax.ShapeDtypeStruct((64, BS, 128), F32)


def cost(flops):
    return pl.CostEstimate(flops=flops, bytes_accessed=1 << 23, transcendentals=0)


def run_fine_product(cols, slot_c, a, pc):
    rows = a.shape[0] * BS
    return pl.pallas_call(
        fine_product,
        out_shape=(pltpu.VMEM((rows, 1024), BF16),) * 2,
        in_specs=[SMEM] * 2 + [HBM] + [VMEM] * 10,
        out_specs=(VMEM, VMEM),
        scratch_shapes=[
            pltpu.VMEM(a.shape, BF16),
            pltpu.VMEM((64, BS, 1024), BF16),
            pltpu.SemaphoreType.DMA,
        ],
        compiler_params=pltpu.CompilerParams(vmem_limit_bytes=28 << 20),
        cost_estimate=cost(2 << 33),
        name="fine_product",
    )(cols, slot_c, a, *pc)


def run_other_half(core, slot_r, hi, lo, pr):
    return pl.pallas_call(
        other_half,
        out_shape=(pltpu.VMEM((2, 512, hi.shape[0]), BF16), HALF),
        in_specs=[SMEM] * 2 + [VMEM] * 6,
        out_specs=(VMEM, VMEM),
        compiler_params=pltpu.CompilerParams(vmem_limit_bytes=28 << 20),
        cost_estimate=cost(1 << 33),
        name="other_half",
    )(core, slot_r, hi, lo, *pr)


def run_own_half(hi, lo, turned):
    return pl.pallas_call(
        own_half,
        out_shape=HALF,
        in_specs=[VMEM] * 3,
        out_specs=VMEM,
        compiler_params=pltpu.CompilerParams(vmem_limit_bytes=28 << 20),
        cost_estimate=cost(1 << 33),
        name="own_half",
    )(hi, lo, turned)


def gather_pieces(piece):
    near, far, beside = together(
        send(piece, REFLECT), send(piece, REFLECT_FAR), send(piece, BESIDE)
    )
    c0 = jnp.concatenate([near, far])
    r0 = jnp.concatenate([piece, beside])
    c1, c2, d0 = together(send(c0, NEXT_X), send(c0, LAST_X), send(c0, OTHER_CORE))
    c3, c4, d1, d2, r0 = together(
        send(c1[:1], NEXT_X), send(c2[1:], LAST_X), send(c1, OTHER_CORE), send(c2, OTHER_CORE), r0
    )
    d3, d4 = send(c3, OTHER_CORE), send(c4, OTHER_CORE)
    r1, r2, r3 = send(r0, NEXT_Z), send(r0, LAST_Z), send(r0, ACROSS_Z)
    return (c0, c1, c2, c3, c4, d0, d1, d2, d3, d4), (r0, r1, r2, r3)


def slots():
    x, yh, core, z, yl = (lax.axis_index(name).astype(jnp.int32) for name in AXES)
    step = jnp.array([0, 0, -1, -1, 1, 1, 2, 2], jnp.int32)
    side = jnp.array([0, 1, 0, 1, 0, 1, 0, 1], jnp.int32)
    mine = 2 * ((2 * z - x - step) % 4) + (yh ^ side)
    slot_c = jnp.concatenate([mine + 8 * core, mine + 8 * (1 - core)])
    slot_r = 2 * ((z + step) % 4) + (yl ^ side)
    return core.reshape(1), slot_c, slot_r


def pack(a_ref, b_ref, out_ref):
    @pl.loop(0, a_ref.shape[0])
    def _(i):
        total = a_ref[i] + b_ref[i]
        largest = jnp.max(jnp.abs(total), axis=0, keepdims=True)
        power = jnp.clip(jnp.ceil(jnp.log2(jnp.maximum(largest, 1e-36))), -110.0, 60.0)
        scaled = jnp.floor(total * jnp.exp2(15.0 - power) + 0.5)
        scaled = jnp.minimum(scaled, 32767.0)
        out_ref[i, :BS, :] = scaled.astype(jnp.int32).astype(jnp.int16)
        power = jnp.broadcast_to(power, (ROWS - BS, 128))
        out_ref[i, BS:, :] = power.astype(jnp.int32).astype(jnp.int16)


def unpack(in_ref, out_ref):
    def step(j, total):
        value = in_ref[j].astype(jnp.int32).astype(F32)
        return total + value[:BS] * jnp.exp2(value[BS : BS + 1] - 15.0)

    out_ref[...] = lax.fori_loop(0, in_ref.shape[0], step, jnp.zeros((BS, 128), F32), unroll=4)


def packed_sum(a, b):
    return pl.pallas_call(
        pack,
        out_shape=jax.ShapeDtypeStruct((64, ROWS, 128), jnp.int16),
        in_specs=[VMEM, VMEM],
        out_specs=VMEM,
        compiler_params=pltpu.CompilerParams(vmem_limit_bytes=8 << 20),
        name="pack",
    )(a, b)


def unpacked_sum(mixed):
    return pl.pallas_call(
        unpack,
        out_shape=jax.ShapeDtypeStruct((BS, 128), F32),
        in_specs=[VMEM],
        out_specs=VMEM,
        compiler_params=pltpu.CompilerParams(vmem_limit_bytes=4 << 20),
        name="unpack",
    )(mixed)


def shards(a_vals, a_cols, p_vals, p_cols):
    ids = jnp.repeat(p_cols.astype(BF16), BS, axis=1)
    blank = jnp.zeros((PAD - 4, 4 * BS), BF16)
    piece = jnp.concatenate([p_vals.reshape(4 * BS, 4 * BS), ids, blank])
    pc, pr = gather_pieces(piece[None])
    core, slot_c, slot_r = slots()
    a = pltpu.with_memory_space_constraint(a_vals[:, 0], pltpu.HBM)
    hi, lo = run_fine_product(a_cols[:, 0], slot_c, a, pc)
    turned, other = run_other_half(core, slot_r, hi, lo, pr)
    met = send(other, OTHER_CORE)
    own = run_own_half(hi, lo, turned)
    packed = packed_sum(own, met)
    mixed = lax.all_to_all(packed, ("x", "yh", "z", "yl"), 0, 0, tiled=True)
    return unpacked_sum(mixed)


def solution(mesh):
    fine = Mesh(mesh.devices.reshape(SIZES), AXES)
    row, col = ("x", "yh", "core"), ("z", "yl")
    in_specs = (
        P(row, col, None, None),
        P(row, col, None),
        P(row + col, None, None),
        P(row + col, None),
    )
    return jax.shard_map(
        shards, mesh=fine, in_specs=in_specs, out_specs=P(row, col), check_vma=False
    )
```

```python
import functools

import jax
import jax.numpy as jnp
from jax import lax
from jax.experimental import pallas as pl
from jax.experimental.pallas import tpu as pltpu
from jax.sharding import Mesh
from jax.sharding import PartitionSpec as P

AXES = ("x", "yh", "core", "z", "yl")
SIZES = (4, 2, 2, 4, 2)
BF16 = jnp.bfloat16
F32 = jnp.float32
BS = 64
ROWS = 72
HALF_ROWS = 136


def linear(place):
    index = 0
    for at, size in zip(place, SIZES):
        index = index * size + at
    return index


def route(target):
    pairs = []
    for x in range(4):
        for yh in range(2):
            for core in range(2):
                for z in range(4):
                    for yl in range(2):
                        to_x, to_y, to_core, to_z = target(x, 2 * yh + yl, core, z)
                        to_x, to_y, to_z = to_x % 4, to_y % 4, to_z % 4
                        to = linear((to_x, to_y // 2, to_core, to_z, to_y % 2))
                        pairs.append((linear((x, yh, core, z, yl)), to))
    return pairs


def swap_y(y):
    return (y % 2) * 2 + y // 2


REFLECT = route(lambda x, y, c, z: (2 * x - z + 2, swap_y(y), c, x))
ACROSS_Y = route(lambda x, y, c, z: (x, y + 2, c, z))
OTHER_CORE = route(lambda x, y, c, z: (x, y, 1 - c, z))
NEXT_X = route(lambda x, y, c, z: (x + 1, y, c, z))
LAST_X = route(lambda x, y, c, z: (x - 1, y, c, z))
NEXT_Z = route(lambda x, y, c, z: (x, y, c, z + 1))
LAST_Z = route(lambda x, y, c, z: (x, y, c, z - 1))
ACROSS_Z = route(lambda x, y, c, z: (x, y, c, z + 2))
BESIDE = route(lambda x, y, c, z: (x, y ^ 1, c, z))


def send(value, pairs):
    return lax.ppermute(value, AXES, pairs)


def together(*values):
    return lax.optimization_barrier(values)


def rows16(row):
    return jnp.broadcast_to(row.astype(F32), (16, 128)).astype(BF16)


def choose(ids, number, values):
    out = [jnp.zeros((16, 128), BF16)] * 4
    for value, at in zip(values, ids):
        hit = at == number
        out = [jnp.where(hit, value[16 * t : 16 * (t + 1)], out[t]) for t in range(4)]
    return jnp.concatenate(out, axis=0)


def swap_halves(v):
    return jnp.concatenate([v[:, BS:], v[:, :BS]], axis=1)


def spread(tile, ids, store):
    low = lax.broadcasted_iota(jnp.int32, (BS, 128), 1) < BS
    low1 = lax.broadcasted_iota(jnp.int32, (1, 128), 1) < BS
    values, where = [], []
    for pair in range(2):
        v = tile[:, 128 * pair : 128 * (pair + 1)].astype(F32)
        r = swap_halves(v)
        d = ids[:, 128 * pair : 128 * (pair + 1)]
        e = swap_halves(d)
        values += [jnp.where(low, v, r).astype(BF16), jnp.where(low, r, v).astype(BF16)]
        for full in (jnp.where(low1, d, e), jnp.where(low1, e, d)):
            where.append(rows16(full - jnp.where(low1, 0.0, 1.0)))
    for g in range(8):
        store(g, choose(where, jnp.asarray(2.0 * g, BF16), values))


def position(name):
    return lax.axis_index(name).astype(jnp.int32)


def flip(bit, number):
    return bit if number == 0 else 1 - bit


NEAR = ((0, 0, 0, 2),)
BEHIND, AHEAD, ACROSS = ((-1, 0, 0, 2),), ((1, 0, 0, 2),), ((0, 1, 0, 2),)
BEHIND2, AHEAD2 = ((-1, 1, 0, 2), (2, 0, 0, 1)), ((1, 1, 0, 2), (2, 0, 1, 1))
BEHIND3, AHEAD3 = ((2, 1, 0, 1),), ((2, 1, 1, 1),)


def place(ref, halves, other, dense):
    x, yh, core, z = (position(name) for name in ("x", "yh", "core", "z"))
    owner = 1 - core if other else core
    base = 0
    for step, side, first, count in halves:
        piece = 2 * jnp.bitwise_and(2 * z + 10 - x - step, 3) + flip(yh, side)
        at = 32 * owner + 4 * piece + 2 * first

        def one(h, base=base, at=at):
            ids = ref[base + h, pl.ds(2 * BS, 8), :].astype(F32)
            for b in range(2):

                def store(g, out):
                    dense[at + 2 * h + b, :, 128 * g : 128 * (g + 1)] = out

                spread(ref[base + h, pl.ds(BS * b, BS), :], ids[b : b + 1], store)

        if count == 1:
            one(0)
        else:
            pl.loop(0, count)(one)
        base += count


def place_all(what, *refs):
    for (halves, other), ref in zip(what, refs):
        place(ref, halves, other, refs[-1])


def fine_product(what, cols_ref, a_hbm, *refs):
    arrays, (dense_in, hi, lo, dense, a_ref, sem) = refs[: len(what)], refs[len(what) :]
    fetch = pltpu.make_async_copy(a_hbm, a_ref, sem)
    fetch.start()
    place_all(what, *arrays, dense)
    fetch.wait()

    @pl.loop(0, a_ref.shape[0])
    def _(i):
        for n in range(4):
            total = None
            for k in range(4):
                tiles = [
                    dense[cols_ref[4 * k + j, i], :, 256 * n : 256 * (n + 1)] for j in range(4)
                ]
                weights = jnp.concatenate(tiles, axis=0)
                left = a_ref[i, :, 256 * k : 256 * (k + 1)]
                part = jnp.dot(left, weights, preferred_element_type=F32)
                total = part if total is None else total + part
            top = total.astype(BF16)
            rows = pl.ds(pl.multiple_of(i * BS, BS), BS)
            hi[rows, 256 * n : 256 * (n + 1)] = top
            lo[rows, 256 * n : 256 * (n + 1)] = (total - top.astype(F32)).astype(BF16)


def turn(ref, h, turned, core, at):
    ids = ref[h, pl.ds(2 * BS, 8), :].astype(F32)
    flipped = ref[h, pl.ds(0, 128), :].astype(F32).T.astype(BF16)
    where, values = [], []
    for m in range(4):
        a = ids[0:1, BS * m : BS * (m + 1)]
        b = ids[1:2, BS * m : BS * (m + 1)]
        where.append(rows16(jnp.concatenate([a, b], axis=1)))
        values.append(flipped[BS * m : BS * (m + 1)])
    for n in range(16):
        out = choose(where, jnp.asarray(float(n), BF16), values)
        slot = core if n % 2 == 0 else 1 - core
        turned[slot, pl.ds(BS * (n // 2), BS), pl.ds(pl.multiple_of(at, 128), 128)] = out


def half_product(turned, slot, hi, lo, out_ref):
    @pl.loop(0, 4)
    def _(n):
        at = pl.ds(pl.multiple_of(256 * n, 256), 256)
        left = turned[slot]
        c = jnp.dot(left, hi[:, at], preferred_element_type=F32)
        c = c + jnp.dot(left, lo[:, at], preferred_element_type=F32)
        for q in range(8):
            for j in range(2):
                out_ref[8 * q + 2 * n + j] = c[BS * q : BS * (q + 1), 128 * j : 128 * (j + 1)]


def other_half(hi, lo, r0, r1, r2, r3, turned, out_ref):
    core, z, yl = (position(name) for name in ("core", "z", "yl"))
    for ref, step in ((r0, 0), (r1, -1), (r2, 1), (r3, 2)):
        for side in range(2):
            at = 256 * (2 * jnp.bitwise_and(z + step + 4, 3) + flip(yl, side))

            @pl.loop(0, 2)
            def _(h):
                turn(ref, 2 * side + h, turned, core, at + 128 * h)

    half_product(turned, 1, hi, lo, out_ref)


def own_half(hi, lo, turned, out_ref):
    half_product(turned, 0, hi, lo, out_ref)


VMEM = pl.BlockSpec(memory_space=pltpu.VMEM)
SMEM = pl.BlockSpec(memory_space=pltpu.SMEM)
HBM = pl.BlockSpec(memory_space=pltpu.HBM)
HALF = jax.ShapeDtypeStruct((64, BS, 128), F32)


def cost(flops):
    return pl.CostEstimate(flops=flops, bytes_accessed=1 << 23, transcendentals=0)


DENSE = pltpu.VMEM((64, BS, 1024), BF16)


def run_place(what, arrays, dense):
    given = () if dense is None else (dense,)
    body = lambda *refs: place_all(what, *refs[: len(what)], refs[-1])
    return pl.pallas_call(
        body,
        out_shape=DENSE,
        in_specs=[VMEM] * (len(arrays) + len(given)),
        out_specs=VMEM,
        input_output_aliases={len(arrays): 0} if given else {},
        compiler_params=pltpu.CompilerParams(vmem_limit_bytes=16 << 20),
        cost_estimate=cost(1 << 30),
        name="place",
    )(*arrays, *given)


def run_fine_product(what, cols, a, arrays, dense):
    rows = a.shape[0] * BS
    return pl.pallas_call(
        functools.partial(fine_product, what),
        out_shape=(pltpu.VMEM((rows, 1024), BF16),) * 2 + (DENSE,),
        in_specs=[SMEM, HBM] + [VMEM] * (len(arrays) + 1),
        out_specs=(VMEM,) * 3,
        scratch_shapes=[pltpu.VMEM(a.shape, BF16), pltpu.SemaphoreType.DMA],
        input_output_aliases={2 + len(arrays): 2},
        compiler_params=pltpu.CompilerParams(vmem_limit_bytes=24 << 20),
        cost_estimate=cost(2 << 33),
        name="fine_product",
    )(cols, a, *arrays, dense)


def run_other_half(hi, lo, pr):
    return pl.pallas_call(
        other_half,
        out_shape=(pltpu.VMEM((2, 512, hi.shape[0]), BF16), HALF),
        in_specs=[VMEM] * 6,
        out_specs=(VMEM, VMEM),
        compiler_params=pltpu.CompilerParams(vmem_limit_bytes=28 << 20),
        cost_estimate=cost(1 << 33),
        name="other_half",
    )(hi, lo, *pr)


def run_own_half(hi, lo, turned):
    return pl.pallas_call(
        own_half,
        out_shape=HALF,
        in_specs=[VMEM] * 3,
        out_specs=VMEM,
        compiler_params=pltpu.CompilerParams(vmem_limit_bytes=28 << 20),
        cost_estimate=cost(1 << 33),
        name="own_half",
    )(hi, lo, turned)


def stamp(cols_ref, vals_ref, out_ref):
    block = lax.broadcasted_iota(jnp.int32, (1, 4 * BS), 1) // BS
    for h in range(2):
        out_ref[h, :BS, :] = vals_ref[2 * h]
        out_ref[h, BS : 2 * BS, :] = vals_ref[2 * h + 1]
        rows = []
        for b in range(2):
            row = jnp.zeros((1, 4 * BS), jnp.int32)
            for m in range(4):
                row = jnp.where(block == m, cols_ref[2 * h + b, m], row)
            rows.append(row)
        rows.append(jnp.zeros((6, 4 * BS), jnp.int32))
        out_ref[h, 2 * BS :, :] = jnp.concatenate(rows).astype(F32).astype(BF16)


def run_stamp(cols, vals):
    return pl.pallas_call(
        stamp,
        out_shape=jax.ShapeDtypeStruct((2, HALF_ROWS, 4 * BS), BF16),
        in_specs=[SMEM, VMEM],
        out_specs=VMEM,
        compiler_params=pltpu.CompilerParams(vmem_limit_bytes=2 << 20),
        name="stamp",
    )(cols, vals)


def fetch_and_multiply(piece, cols, a):
    near, beside = together(send(piece, REFLECT), send(piece, BESIDE))
    b1, a1, f, e0, r0, dense = together(
        send(near, NEXT_X),
        send(near, LAST_X),
        send(near, ACROSS_Y),
        send(near, OTHER_CORE),
        jnp.concatenate([piece, beside]),
        run_place(((NEAR, False),), (near,), None),
    )
    what = ((BEHIND, False), (AHEAD, False), (ACROSS, False), (NEAR, True))
    b2, a2, e1, e2, e3, dense = together(
        send(jnp.concatenate([f, b1[:1]]), NEXT_X),
        send(jnp.concatenate([f, a1[1:]]), LAST_X),
        send(b1, OTHER_CORE),
        send(a1, OTHER_CORE),
        send(f, OTHER_CORE),
        run_place(what, (b1, a1, f, e0), dense),
    )
    what = ((BEHIND2, False), (AHEAD2, False), (BEHIND, True), (AHEAD, True), (ACROSS, True))
    b3, a3, e4, e5, dense = together(
        send(b2[:1], NEXT_X),
        send(a2[1:2], LAST_X),
        send(b2, OTHER_CORE),
        send(a2, OTHER_CORE),
        run_place(what, (b2, a2, e1, e2, e3), dense),
    )
    what = ((BEHIND3, False), (AHEAD3, False), (BEHIND2, True), (AHEAD2, True))
    e6, e7 = send(b3, OTHER_CORE), send(a3, OTHER_CORE)
    r1, r2, r3 = send(r0, NEXT_Z), send(r0, LAST_Z), send(r0, ACROSS_Z)
    dense = run_place(what, (b3, a3, e4, e5), dense)
    what = ((BEHIND3, True), (AHEAD3, True))
    hi, lo, dense = run_fine_product(what, cols, a, (e6, e7), dense)
    return hi, lo, (r0, r1, r2, r3)


def pack(a_ref, b_ref, out_ref):
    @pl.loop(0, a_ref.shape[0])
    def _(i):
        total = a_ref[i] + b_ref[i]
        largest = jnp.max(jnp.abs(total), axis=0, keepdims=True)
        power = jnp.clip(jnp.ceil(jnp.log2(jnp.maximum(largest, 1e-36))), -110.0, 60.0)
        scaled = jnp.floor(total * jnp.exp2(15.0 - power) + 0.5)
        scaled = jnp.minimum(scaled, 32767.0)
        out_ref[i, :BS, :] = scaled.astype(jnp.int32).astype(jnp.int16)
        power = jnp.broadcast_to(power, (ROWS - BS, 128))
        out_ref[i, BS:, :] = power.astype(jnp.int32).astype(jnp.int16)


def unpack(in_ref, out_ref):
    def step(j, total):
        value = in_ref[j].astype(jnp.int32).astype(F32)
        return total + value[:BS] * jnp.exp2(value[BS : BS + 1] - 15.0)

    out_ref[...] = lax.fori_loop(0, in_ref.shape[0], step, jnp.zeros((BS, 128), F32), unroll=4)


def packed_sum(a, b):
    return pl.pallas_call(
        pack,
        out_shape=jax.ShapeDtypeStruct((64, ROWS, 128), jnp.int16),
        in_specs=[VMEM, VMEM],
        out_specs=VMEM,
        compiler_params=pltpu.CompilerParams(vmem_limit_bytes=8 << 20),
        name="pack",
    )(a, b)


def unpacked_sum(mixed):
    return pl.pallas_call(
        unpack,
        out_shape=jax.ShapeDtypeStruct((BS, 128), F32),
        in_specs=[VMEM],
        out_specs=VMEM,
        compiler_params=pltpu.CompilerParams(vmem_limit_bytes=4 << 20),
        name="unpack",
    )(mixed)


def shards(a_vals, a_cols, p_vals, p_cols):
    a = pltpu.with_memory_space_constraint(a_vals[:, 0], pltpu.HBM)
    piece = run_stamp(p_cols, p_vals)
    hi, lo, pr = fetch_and_multiply(piece, a_cols[:, 0].T, a)
    turned, other = run_other_half(hi, lo, pr)
    met = send(other, OTHER_CORE)
    own = run_own_half(hi, lo, turned)
    packed = packed_sum(own, met)
    mixed = lax.all_to_all(packed, ("x", "yh", "z", "yl"), 0, 0, tiled=True)
    return unpacked_sum(mixed)


def solution(mesh):
    fine = Mesh(mesh.devices.reshape(SIZES), AXES)
    row, col = ("x", "yh", "core"), ("z", "yl")
    in_specs = (
        P(row, col, None, None),
        P(row, col, None),
        P(row + col, None, None),
        P(row + col, None),
    )
    return jax.shard_map(
        shards, mesh=fine, in_specs=in_specs, out_specs=P(row, col), check_vma=False
    )
```

```python
import functools

import jax
import jax.numpy as jnp
from jax import lax
from jax.experimental import pallas as pl
from jax.experimental.pallas import tpu as pltpu
from jax.sharding import Mesh
from jax.sharding import PartitionSpec as P

AXES = ("x", "yh", "core", "z", "yl")
SIZES = (4, 2, 2, 4, 2)
BF16 = jnp.bfloat16
F32 = jnp.float32
BS = 64
ROWS = 72
HALF_ROWS = 136


def linear(place):
    index = 0
    for at, size in zip(place, SIZES):
        index = index * size + at
    return index


def route(target):
    pairs = []
    for x in range(4):
        for yh in range(2):
            for core in range(2):
                for z in range(4):
                    for yl in range(2):
                        to_x, to_y, to_core, to_z = target(x, 2 * yh + yl, core, z)
                        to_x, to_y, to_z = to_x % 4, to_y % 4, to_z % 4
                        to = linear((to_x, to_y // 2, to_core, to_z, to_y % 2))
                        pairs.append((linear((x, yh, core, z, yl)), to))
    return pairs


def swap_y(y):
    return (y % 2) * 2 + y // 2


REFLECT = route(lambda x, y, c, z: (2 * x - z + 2, swap_y(y), c, x))
ACROSS_Y = route(lambda x, y, c, z: (x, y + 2, c, z))
OTHER_CORE = route(lambda x, y, c, z: (x, y, 1 - c, z))
NEXT_X = route(lambda x, y, c, z: (x + 1, y, c, z))
LAST_X = route(lambda x, y, c, z: (x - 1, y, c, z))
NEXT_Z = route(lambda x, y, c, z: (x, y, c, z + 1))
LAST_Z = route(lambda x, y, c, z: (x, y, c, z - 1))
ACROSS_Z = route(lambda x, y, c, z: (x, y, c, z + 2))
BESIDE = route(lambda x, y, c, z: (x, y ^ 1, c, z))


def send(value, pairs):
    return lax.ppermute(value, AXES, pairs)


def together(*values):
    return lax.optimization_barrier(values)


def rows16(row):
    return jnp.broadcast_to(row.astype(F32), (16, 128)).astype(BF16)


def choose(ids, number, values):
    out = [jnp.zeros((16, 128), BF16)] * 4
    for value, at in zip(values, ids):
        hit = at == number
        out = [jnp.where(hit, value[16 * t : 16 * (t + 1)], out[t]) for t in range(4)]
    return jnp.concatenate(out, axis=0)


def swap_halves(v):
    return jnp.concatenate([v[:, BS:], v[:, :BS]], axis=1)


def spread(tile, ids, store):
    low = lax.broadcasted_iota(jnp.int32, (BS, 128), 1) < BS
    low1 = lax.broadcasted_iota(jnp.int32, (1, 128), 1) < BS
    values, where = [], []
    for pair in range(2):
        v = tile[:, 128 * pair : 128 * (pair + 1)].astype(F32)
        r = swap_halves(v)
        d = ids[:, 128 * pair : 128 * (pair + 1)]
        e = swap_halves(d)
        values += [jnp.where(low, v, r).astype(BF16), jnp.where(low, r, v).astype(BF16)]
        for full in (jnp.where(low1, d, e), jnp.where(low1, e, d)):
            where.append(rows16(full - jnp.where(low1, 0.0, 1.0)))
    for g in range(8):
        store(g, choose(where, jnp.asarray(2.0 * g, BF16), values))


def position(name):
    return lax.axis_index(name).astype(jnp.int32)


def flip(bit, number):
    return bit if number == 0 else 1 - bit


NEAR = ((0, 0, 0, 2),)
BEHIND, AHEAD, ACROSS = ((-1, 0, 0, 2),), ((1, 0, 0, 2),), ((0, 1, 0, 2),)
BEHIND2, AHEAD2 = ((-1, 1, 0, 2), (2, 0, 0, 1)), ((1, 1, 0, 2), (2, 0, 1, 1))
BEHIND3, AHEAD3 = ((2, 1, 0, 1),), ((2, 1, 1, 1),)


def place(ref, halves, other, dense):
    x, yh, core, z = (position(name) for name in ("x", "yh", "core", "z"))
    owner = 1 - core if other else core
    base = 0
    for step, side, first, count in halves:
        piece = 2 * jnp.bitwise_and(2 * z + 10 - x - step, 3) + flip(yh, side)
        at = 32 * owner + 4 * piece + 2 * first

        def one(h, base=base, at=at):
            ids = ref[base + h, pl.ds(2 * BS, 8), :].astype(F32)
            for b in range(2):

                def store(g, out):
                    dense[at + 2 * h + b, :, 128 * g : 128 * (g + 1)] = out

                spread(ref[base + h, pl.ds(BS * b, BS), :], ids[b : b + 1], store)

        if count == 1:
            one(0)
        else:
            pl.loop(0, count)(one)
        base += count


def place_all(what, *refs):
    for (halves, other), ref in zip(what, refs):
        place(ref, halves, other, refs[-1])


def fine_product(what, cols_ref, a_ref, *refs):
    arrays, (dense_in, hi, lo, dense) = refs[: len(what)], refs[len(what) :]
    place_all(what, *arrays, dense)

    @pl.loop(0, a_ref.shape[0])
    def _(i):
        for n in range(4):
            total = None
            for k in range(4):
                tiles = [
                    dense[cols_ref[4 * k + j, i], :, 256 * n : 256 * (n + 1)] for j in range(4)
                ]
                weights = jnp.concatenate(tiles, axis=0)
                left = a_ref[i, :, 256 * k : 256 * (k + 1)]
                part = jnp.dot(left, weights, preferred_element_type=F32)
                total = part if total is None else total + part
            top = total.astype(BF16)
            rows = pl.ds(pl.multiple_of(i * BS, BS), BS)
            hi[rows, 256 * n : 256 * (n + 1)] = top
            lo[rows, 256 * n : 256 * (n + 1)] = (total - top.astype(F32)).astype(BF16)


def turn(ref, h, turned, core, at):
    ids = ref[h, pl.ds(2 * BS, 8), :].astype(F32)
    flipped = ref[h, pl.ds(0, 128), :].astype(F32).T.astype(BF16)
    where, values = [], []
    for m in range(4):
        a = ids[0:1, BS * m : BS * (m + 1)]
        b = ids[1:2, BS * m : BS * (m + 1)]
        where.append(rows16(jnp.concatenate([a, b], axis=1)))
        values.append(flipped[BS * m : BS * (m + 1)])
    for n in range(16):
        out = choose(where, jnp.asarray(float(n), BF16), values)
        slot = core if n % 2 == 0 else 1 - core
        turned[slot, pl.ds(BS * (n // 2), BS), pl.ds(pl.multiple_of(at, 128), 128)] = out


def half_product(turned, slot, hi, lo, out_ref):
    @pl.loop(0, 4)
    def _(n):
        at = pl.ds(pl.multiple_of(256 * n, 256), 256)
        left = turned[slot]
        c = jnp.dot(left, hi[:, at], preferred_element_type=F32)
        c = c + jnp.dot(left, lo[:, at], preferred_element_type=F32)
        for q in range(8):
            for j in range(2):
                out_ref[8 * q + 2 * n + j] = c[BS * q : BS * (q + 1), 128 * j : 128 * (j + 1)]


def other_half(hi, lo, r0, r1, r2, r3, turned, out_ref):
    core, z, yl = (position(name) for name in ("core", "z", "yl"))
    for ref, step in ((r0, 0), (r1, -1), (r2, 1), (r3, 2)):
        for side in range(2):
            at = 256 * (2 * jnp.bitwise_and(z + step + 4, 3) + flip(yl, side))

            @pl.loop(0, 2)
            def _(h):
                turn(ref, 2 * side + h, turned, core, at + 128 * h)

    half_product(turned, 1, hi, lo, out_ref)


def own_half(hi, lo, turned, out_ref):
    half_product(turned, 0, hi, lo, out_ref)


def in_hbm(v):
    return pltpu.with_memory_space_constraint(v, pltpu.HBM)


VMEM = pl.BlockSpec(memory_space=pltpu.VMEM)
SMEM = pl.BlockSpec(memory_space=pltpu.SMEM)
HBM = pl.BlockSpec(memory_space=pltpu.HBM)
HALF = jax.ShapeDtypeStruct((64, BS, 128), F32)


def cost(flops):
    return pl.CostEstimate(flops=flops, bytes_accessed=1 << 23, transcendentals=0)


DENSE = pltpu.VMEM((64, BS, 1024), BF16)


def run_place(what, arrays, dense, a=None):
    given = () if dense is None else (dense,)
    fetched = () if a is None else (a,)
    count = len(arrays) + len(given)

    def body(*refs):
        if a is None:
            place_all(what, *refs[: len(what)], refs[-1])
        else:
            fetch = pltpu.make_async_copy(refs[count], refs[count + 2], refs[-1])
            fetch.start()
            place_all(what, *refs[: len(what)], refs[count + 1])
            fetch.wait()

    out = pl.pallas_call(
        body,
        out_shape=(DENSE,) + tuple(pltpu.VMEM(v.shape, v.dtype) for v in fetched),
        in_specs=[VMEM] * count + [HBM] * len(fetched),
        out_specs=(VMEM,) * (1 + len(fetched)),
        scratch_shapes=[pltpu.SemaphoreType.DMA] * len(fetched),
        input_output_aliases={len(arrays): 0} if given else {},
        compiler_params=pltpu.CompilerParams(vmem_limit_bytes=16 << 20),
        cost_estimate=cost(1 << 30),
        name="place",
    )(*arrays, *given, *fetched)
    return out if fetched else out[0]


def run_fine_product(what, cols, a, arrays, dense):
    rows = a.shape[0] * BS
    return pl.pallas_call(
        functools.partial(fine_product, what),
        out_shape=(pltpu.VMEM((rows, 1024), BF16),) * 2 + (DENSE,),
        in_specs=[SMEM] + [VMEM] * (len(arrays) + 2),
        out_specs=(VMEM,) * 3,
        input_output_aliases={2 + len(arrays): 2},
        compiler_params=pltpu.CompilerParams(vmem_limit_bytes=16 << 20),
        cost_estimate=cost(2 << 33),
        name="fine_product",
    )(cols, a, *arrays, dense)


def run_other_half(hi, lo, pr):
    return pl.pallas_call(
        other_half,
        out_shape=(pltpu.VMEM((2, 512, hi.shape[0]), BF16), HALF),
        in_specs=[VMEM] * 6,
        out_specs=(VMEM, VMEM),
        compiler_params=pltpu.CompilerParams(vmem_limit_bytes=28 << 20),
        cost_estimate=cost(1 << 33),
        name="other_half",
    )(hi, lo, *pr)


def run_own_half(hi, lo, turned):
    return pl.pallas_call(
        own_half,
        out_shape=HALF,
        in_specs=[VMEM] * 3,
        out_specs=VMEM,
        compiler_params=pltpu.CompilerParams(vmem_limit_bytes=28 << 20),
        cost_estimate=cost(1 << 33),
        name="own_half",
    )(hi, lo, turned)


def stamp(cols_ref, vals_ref, out_ref, sems):
    copies = []
    for b in range(4):
        to = out_ref.at[b // 2, pl.ds(BS * (b % 2), BS)]
        copies.append(pltpu.make_async_copy(vals_ref.at[b], to, sems.at[b]))
        copies[b].start()
    block = lax.broadcasted_iota(jnp.int32, (1, 4 * BS), 1) // BS
    for h in range(2):
        rows = []
        for b in range(2):
            row = jnp.zeros((1, 4 * BS), jnp.int32)
            for m in range(4):
                row = jnp.where(block == m, cols_ref[2 * h + b, m], row)
            rows.append(row)
        rows.append(jnp.zeros((6, 4 * BS), jnp.int32))
        out_ref[h, 2 * BS :, :] = jnp.concatenate(rows).astype(F32).astype(BF16)
    for copy in copies:
        copy.wait()


def run_stamp(cols, vals):
    return pl.pallas_call(
        stamp,
        out_shape=jax.ShapeDtypeStruct((2, HALF_ROWS, 4 * BS), BF16),
        in_specs=[SMEM, HBM],
        out_specs=VMEM,
        scratch_shapes=[pltpu.SemaphoreType.DMA((4,))],
        compiler_params=pltpu.CompilerParams(vmem_limit_bytes=2 << 20),
        name="stamp",
    )(in_hbm(cols), in_hbm(vals))


def fetch_and_multiply(piece, cols, a):
    near, beside = together(send(piece, REFLECT), send(piece, BESIDE))
    b1, a1, f, r0, dense = together(
        send(near, NEXT_X),
        send(near, LAST_X),
        send(near, ACROSS_Y),
        jnp.concatenate([piece, beside]),
        run_place(((NEAR, False),), (near,), None),
    )
    what = ((BEHIND, False), (AHEAD, False), (ACROSS, False))
    b2, a2, e1, r0, dense = together(
        send(jnp.concatenate([f, b1[:1]]), NEXT_X),
        send(jnp.concatenate([f, a1[1:]]), LAST_X),
        send(jnp.concatenate([near, b1, a1, f]), OTHER_CORE),
        r0,
        run_place(what, (b1, a1, f), dense),
    )
    what = ((BEHIND2, False), (AHEAD2, False), (NEAR + BEHIND + AHEAD + ACROSS, True))
    b3, a3, e2, r0, (dense, a) = together(
        send(b2[:1], NEXT_X),
        send(a2[1:2], LAST_X),
        send(jnp.concatenate([b2, a2]), OTHER_CORE),
        r0,
        run_place(what, (b2, a2, e1), dense, a),
    )
    e3 = send(jnp.concatenate([b3, a3]), OTHER_CORE)
    r1, r2, r3 = send(r0, NEXT_Z), send(r0, LAST_Z), send(r0, ACROSS_Z)
    what = ((BEHIND3, False), (AHEAD3, False), (BEHIND2 + AHEAD2, True))
    dense = run_place(what, (b3, a3, e2), dense)
    what = ((BEHIND3 + AHEAD3, True),)
    hi, lo, dense = run_fine_product(what, cols, a, (e3,), dense)
    return hi, lo, (r0, r1, r2, r3)


def pack(a_ref, b_ref, out_ref):
    @pl.loop(0, a_ref.shape[0])
    def _(i):
        total = a_ref[i] + b_ref[i]
        largest = jnp.max(jnp.abs(total), axis=0, keepdims=True)
        power = jnp.clip(jnp.ceil(jnp.log2(jnp.maximum(largest, 1e-36))), -110.0, 60.0)
        scaled = jnp.floor(total * jnp.exp2(15.0 - power) + 0.5)
        scaled = jnp.minimum(scaled, 32767.0)
        out_ref[i, :BS, :] = scaled.astype(jnp.int32).astype(jnp.int16)
        power = jnp.broadcast_to(power, (ROWS - BS, 128))
        out_ref[i, BS:, :] = power.astype(jnp.int32).astype(jnp.int16)


def unpack(in_ref, out_ref):
    def step(j, total):
        value = in_ref[j].astype(jnp.int32).astype(F32)
        return total + value[:BS] * jnp.exp2(value[BS : BS + 1] - 15.0)

    out_ref[...] = lax.fori_loop(0, in_ref.shape[0], step, jnp.zeros((BS, 128), F32), unroll=4)


def packed_sum(a, b):
    return pl.pallas_call(
        pack,
        out_shape=jax.ShapeDtypeStruct((64, ROWS, 128), jnp.int16),
        in_specs=[VMEM, VMEM],
        out_specs=VMEM,
        compiler_params=pltpu.CompilerParams(vmem_limit_bytes=8 << 20),
        name="pack",
    )(a, b)


def unpacked_sum(mixed):
    return pl.pallas_call(
        unpack,
        out_shape=jax.ShapeDtypeStruct((BS, 128), F32),
        in_specs=[VMEM],
        out_specs=VMEM,
        compiler_params=pltpu.CompilerParams(vmem_limit_bytes=4 << 20),
        name="unpack",
    )(mixed)


def shards(a_vals, a_cols, p_vals, p_cols):
    a = in_hbm(a_vals[:, 0])
    piece = run_stamp(p_cols, p_vals)
    hi, lo, pr = fetch_and_multiply(piece, a_cols[:, 0].T, a)
    turned, other = run_other_half(hi, lo, pr)
    met = send(other, OTHER_CORE)
    own = run_own_half(hi, lo, turned)
    packed = packed_sum(own, met)
    mixed = lax.all_to_all(packed, ("x", "yh", "z", "yl"), 0, 0, tiled=True)
    return unpacked_sum(mixed)


def solution(mesh):
    fine = Mesh(mesh.devices.reshape(SIZES), AXES)
    row, col = ("x", "yh", "core"), ("z", "yl")
    in_specs = (
        P(row, col, None, None),
        P(row, col, None),
        P(row + col, None, None),
        P(row + col, None),
    )
    return jax.shard_map(
        shards, mesh=fine, in_specs=in_specs, out_specs=P(row, col), check_vma=False
    )
```

```python
import functools

import jax
import jax.numpy as jnp
from jax import lax
from jax.experimental import pallas as pl
from jax.experimental.pallas import tpu as pltpu
from jax.sharding import Mesh
from jax.sharding import PartitionSpec as P


AXES = ("x", "yh", "core", "z", "yl")
SIZES = (4, 2, 2, 4, 2)
BF16 = jnp.bfloat16
F32 = jnp.float32
BS = 64
ROWS = 72
HALF_ROWS = 136


def linear(place):
    index = 0
    for at, size in zip(place, SIZES):
        index = index * size + at
    return index


def route(target):
    pairs = []
    for x in range(4):
        for yh in range(2):
            for core in range(2):
                for z in range(4):
                    for yl in range(2):
                        to_x, to_y, to_core, to_z = target(x, 2 * yh + yl, core, z)
                        to_x, to_y, to_z = to_x % 4, to_y % 4, to_z % 4
                        to = linear((to_x, to_y // 2, to_core, to_z, to_y % 2))
                        pairs.append((linear((x, yh, core, z, yl)), to))
    return pairs


def swap_y(y):
    return (y % 2) * 2 + y // 2


REFLECT = route(lambda x, y, c, z: (2 * x - z + 2, swap_y(y), c, x))
ACROSS_Y = route(lambda x, y, c, z: (x, y + 2, c, z))
OTHER_CORE = route(lambda x, y, c, z: (x, y, 1 - c, z))
NEXT_X = route(lambda x, y, c, z: (x + 1, y, c, z))
LAST_X = route(lambda x, y, c, z: (x - 1, y, c, z))
NEXT_Z = route(lambda x, y, c, z: (x, y, c, z + 1))
LAST_Z = route(lambda x, y, c, z: (x, y, c, z - 1))
ACROSS_Z = route(lambda x, y, c, z: (x, y, c, z + 2))
BESIDE = route(lambda x, y, c, z: (x, y ^ 1, c, z))


def send(value, pairs):
    return lax.ppermute(value, AXES, pairs)


def together(*values):
    return lax.optimization_barrier(values)


def rows16(row):
    return jnp.broadcast_to(row.astype(F32), (16, 128)).astype(BF16)


def choose(ids, number, values):
    out = [jnp.zeros((16, 128), BF16)] * 4
    for value, at in zip(values, ids):
        hit = at == number
        out = [jnp.where(hit, value[16 * t : 16 * (t + 1)], out[t]) for t in range(4)]
    return jnp.concatenate(out, axis=0)


def swap_halves(v):
    return jnp.concatenate([v[:, BS:], v[:, :BS]], axis=1)


def meet(first, free, last):
    fixed = together(*first, *last)
    return fixed[: len(first)] + free + fixed[len(first) :]


def spread(tile, ids, store):
    low = lax.broadcasted_iota(jnp.int32, (BS, 128), 1) < BS
    low1 = lax.broadcasted_iota(jnp.int32, (1, 128), 1) < BS
    values, where = [], []
    for pair in range(2):
        v = tile[:, 128 * pair : 128 * (pair + 1)].astype(F32)
        r = swap_halves(v)
        d = ids[:, 128 * pair : 128 * (pair + 1)]
        e = swap_halves(d)
        values += [jnp.where(low, v, r).astype(BF16), jnp.where(low, r, v).astype(BF16)]
        for full in (jnp.where(low1, d, e), jnp.where(low1, e, d)):
            where.append(rows16(full - jnp.where(low1, 0.0, 1.0)))
    for g in range(8):
        store(g, choose(where, jnp.asarray(2.0 * g, BF16), values))


def position(name):
    return lax.axis_index(name).astype(jnp.int32)


def flip(bit, number):
    return bit if number == 0 else 1 - bit


NEAR = ((0, 0, 0, 2),)
BEHIND, AHEAD, ACROSS = ((-1, 0, 0, 2),), ((1, 0, 0, 2),), ((0, 1, 0, 2),)
BEHIND2, AHEAD2 = ((-1, 1, 0, 2), (2, 0, 0, 1)), ((1, 1, 0, 2), (2, 0, 1, 1))
BEHIND3, AHEAD3 = ((2, 1, 0, 1),), ((2, 1, 1, 1),)


def place(ref, halves, other, dense):
    x, yh, core, z = (position(name) for name in ("x", "yh", "core", "z"))
    owner = 1 - core if other else core
    base = 0
    for step, side, first, count in halves:
        piece = 2 * jnp.bitwise_and(2 * z + 10 - x - step, 3) + flip(yh, side)
        at = 32 * owner + 4 * piece + 2 * first

        def one(h, base=base, at=at):
            ids = ref[base + h, pl.ds(2 * BS, 8), :].astype(F32)
            for b in range(2):

                def store(g, out):
                    dense[at + 2 * h + b, :, 128 * g : 128 * (g + 1)] = out

                spread(ref[base + h, pl.ds(BS * b, BS), :], ids[b : b + 1], store)

        if count == 1:
            one(0)
        else:
            pl.loop(0, count)(one)
        base += count


def place_all(what, *refs):
    for (halves, other), ref in zip(what, refs):
        place(ref, halves, other, refs[-1])


def fine_product(what, cols_ref, a_ref, *refs):
    arrays, (dense_in, hi, lo, dense) = refs[: len(what)], refs[len(what) :]
    place_all(what, *arrays, dense)

    @pl.loop(0, a_ref.shape[0])
    def _(i):
        for n in range(4):
            total = None
            for k in range(4):
                tiles = [
                    dense[cols_ref[4 * k + j, i], :, 256 * n : 256 * (n + 1)] for j in range(4)
                ]
                weights = jnp.concatenate(tiles, axis=0)
                left = a_ref[i, :, 256 * k : 256 * (k + 1)]
                part = jnp.dot(left, weights, preferred_element_type=F32)
                total = part if total is None else total + part
            top = total.astype(BF16)
            rows = pl.ds(pl.multiple_of(i * BS, BS), BS)
            hi[rows, 256 * n : 256 * (n + 1)] = top
            lo[rows, 256 * n : 256 * (n + 1)] = (total - top.astype(F32)).astype(BF16)


def turn(ref, h, turned, core, at):
    ids = ref[h, pl.ds(2 * BS, 8), :].astype(F32)
    flipped = ref[h, pl.ds(0, 128), :].astype(F32).T.astype(BF16)
    where, values = [], []
    for m in range(4):
        a = ids[0:1, BS * m : BS * (m + 1)]
        b = ids[1:2, BS * m : BS * (m + 1)]
        where.append(rows16(jnp.concatenate([a, b], axis=1)))
        values.append(flipped[BS * m : BS * (m + 1)])
    for n in range(16):
        out = choose(where, jnp.asarray(float(n), BF16), values)
        slot = core if n % 2 == 0 else 1 - core
        turned[slot, pl.ds(BS * (n // 2), BS), pl.ds(pl.multiple_of(at, 128), 128)] = out


def half_product(turned, slot, hi, lo, out_ref):
    @pl.loop(0, 4)
    def _(n):
        at = pl.ds(pl.multiple_of(256 * n, 256), 256)
        left = turned[slot]
        c = jnp.dot(left, hi[:, at], preferred_element_type=F32)
        c = c + jnp.dot(left, lo[:, at], preferred_element_type=F32)
        for q in range(8):
            for j in range(2):
                out_ref[8 * q + 2 * n + j] = c[BS * q : BS * (q + 1), 128 * j : 128 * (j + 1)]


def turn_line(ref, side, turned):
    core, z, yl = (position(name) for name in ("core", "z", "yl"))
    for ring, step in enumerate((0, -1, 1, 2)):
        at = 256 * (2 * jnp.bitwise_and(z + step + 4, 3) + flip(yl, side))

        @pl.loop(0, 2)
        def _(h):
            turn(ref, 2 * ring + h, turned, core, at + 128 * h)


def turn_own(line, turned):
    turn_line(line, 0, turned)


def other_half(hi, lo, beside, turned_in, turned, out_ref):
    turn_line(beside, 1, turned)
    half_product(turned, 1, hi, lo, out_ref)


def own_half(hi, lo, turned, out_ref):
    half_product(turned, 0, hi, lo, out_ref)


def in_hbm(v):
    return pltpu.with_memory_space_constraint(v, pltpu.HBM)


VMEM = pl.BlockSpec(memory_space=pltpu.VMEM)
SMEM = pl.BlockSpec(memory_space=pltpu.SMEM)
HBM = pl.BlockSpec(memory_space=pltpu.HBM)
HALF = jax.ShapeDtypeStruct((64, BS, 128), F32)


def cost(flops):
    return pl.CostEstimate(flops=flops, bytes_accessed=1 << 23, transcendentals=0)


DENSE = pltpu.VMEM((64, BS, 1024), BF16)


def run_place(what, arrays, dense, a=None):
    given = () if dense is None else (dense,)
    fetched = () if a is None else (a,)
    count = len(arrays) + len(given)

    def body(*refs):
        if a is None:
            place_all(what, *refs[: len(what)], refs[-1])
        else:
            fetch = pltpu.make_async_copy(refs[count], refs[count + 2], refs[-1])
            fetch.start()
            place_all(what, *refs[: len(what)], refs[count + 1])
            fetch.wait()

    call = pl.pallas_call(
        body,
        out_shape=(DENSE,) + tuple(pltpu.VMEM(v.shape, v.dtype) for v in fetched),
        in_specs=[VMEM] * count + [HBM] * len(fetched),
        out_specs=(VMEM,) * (1 + len(fetched)),
        scratch_shapes=[pltpu.SemaphoreType.DMA] * len(fetched),
        input_output_aliases={len(arrays): 0} if given else {},
        compiler_params=pltpu.CompilerParams(vmem_limit_bytes=16 << 20),
        cost_estimate=cost(1 << 30),
    )
    out = call(*arrays, *given, *fetched)
    return out if fetched else out[0]


def run_fine_product(what, cols, a, arrays, dense):
    rows = a.shape[0] * BS
    return pl.pallas_call(
        functools.partial(fine_product, what),
        out_shape=(pltpu.VMEM((rows, 1024), BF16),) * 2 + (DENSE,),
        in_specs=[SMEM] + [VMEM] * (len(arrays) + 2),
        out_specs=(VMEM,) * 3,
        input_output_aliases={2 + len(arrays): 2},
        compiler_params=pltpu.CompilerParams(vmem_limit_bytes=16 << 20),
        cost_estimate=cost(2 << 33),
        name="fine_product",
    )(cols, a, *arrays, dense)


def run_turn(line):
    return pl.pallas_call(
        turn_own,
        out_shape=pltpu.VMEM((2, 512, 2048), BF16),
        in_specs=[VMEM],
        out_specs=VMEM,
        compiler_params=pltpu.CompilerParams(vmem_limit_bytes=8 << 20),
        cost_estimate=cost(1 << 30),
        name="turn",
    )(line)


def run_other_half(hi, lo, beside, turned):
    return pl.pallas_call(
        other_half,
        out_shape=(pltpu.VMEM(turned.shape, BF16), HALF),
        in_specs=[VMEM] * 4,
        out_specs=(VMEM, VMEM),
        input_output_aliases={3: 0},
        compiler_params=pltpu.CompilerParams(vmem_limit_bytes=16 << 20),
        cost_estimate=cost(1 << 33),
        name="other_half",
    )(hi, lo, beside, turned)


def run_own_half(hi, lo, turned):
    return pl.pallas_call(
        own_half,
        out_shape=HALF,
        in_specs=[VMEM] * 3,
        out_specs=VMEM,
        compiler_params=pltpu.CompilerParams(vmem_limit_bytes=16 << 20),
        cost_estimate=cost(1 << 33),
        name="own_half",
    )(hi, lo, turned)


def stamp(cols_ref, vals_ref, out_ref, sems):
    copies = []
    for b in range(4):
        to = out_ref.at[b // 2, pl.ds(BS * (b % 2), BS)]
        copies.append(pltpu.make_async_copy(vals_ref.at[b], to, sems.at[b]))
        copies[b].start()
    block = lax.broadcasted_iota(jnp.int32, (1, 4 * BS), 1) // BS
    for h in range(2):
        rows = []
        for b in range(2):
            row = jnp.zeros((1, 4 * BS), jnp.int32)
            for m in range(4):
                row = jnp.where(block == m, cols_ref[2 * h + b, m], row)
            rows.append(row)
        rows.append(jnp.zeros((6, 4 * BS), jnp.int32))
        out_ref[h, 2 * BS :, :] = jnp.concatenate(rows).astype(F32).astype(BF16)
    for copy in copies:
        copy.wait()


def run_stamp(cols, vals):
    return pl.pallas_call(
        stamp,
        out_shape=jax.ShapeDtypeStruct((2, HALF_ROWS, 4 * BS), BF16),
        in_specs=[SMEM, HBM],
        out_specs=VMEM,
        scratch_shapes=[pltpu.SemaphoreType.DMA((4,))],
        compiler_params=pltpu.CompilerParams(vmem_limit_bytes=2 << 20),
        name="stamp",
    )(in_hbm(cols), in_hbm(vals))


def fetch_and_multiply(piece, cols, a):
    (near,) = together(send(piece, REFLECT))
    b1, a1, f, z1, z2, z3, dense = meet(
        (send(near, NEXT_X), send(near, LAST_X), send(near, ACROSS_Y)),
        (send(piece, NEXT_Z), send(piece, LAST_Z), send(piece, ACROSS_Z)),
        (run_place(((NEAR, False),), (near,), None),),
    )
    what = ((BEHIND, False), (AHEAD, False), (ACROSS, False))
    line = jnp.concatenate([piece, z1, z2, z3])
    b2, a2, e1, line, dense, turned = together(
        send(jnp.concatenate([f, b1[:1]]), NEXT_X),
        send(jnp.concatenate([f, a1[1:]]), LAST_X),
        send(jnp.concatenate([near, b1, a1, f]), OTHER_CORE),
        line,
        run_place(what, (b1, a1, f), dense),
        run_turn(line),
    )
    what = ((BEHIND2, False), (AHEAD2, False), (NEAR + BEHIND + AHEAD + ACROSS, True))
    beside = send(line, BESIDE)
    b3, a3, e2, (dense, a) = together(
        send(b2[:1], NEXT_X),
        send(a2[1:2], LAST_X),
        send(jnp.concatenate([b2, a2]), OTHER_CORE),
        run_place(what, (b2, a2, e1), dense, a),
    )
    e3 = send(jnp.concatenate([b3, a3]), OTHER_CORE)
    what = ((BEHIND3, False), (AHEAD3, False), (BEHIND2 + AHEAD2, True))
    dense = run_place(what, (b3, a3, e2), dense)
    what = ((BEHIND3 + AHEAD3, True),)
    hi, lo, dense = run_fine_product(what, cols, a, (e3,), dense)
    return hi, lo, turned, beside


def pack(a_ref, b_ref, out_ref):
    @pl.loop(0, a_ref.shape[0])
    def _(i):
        total = a_ref[i] + b_ref[i]
        largest = jnp.max(jnp.abs(total), axis=0, keepdims=True)
        power = jnp.clip(jnp.ceil(jnp.log2(jnp.maximum(largest, 1e-36))), -110.0, 60.0)
        scaled = jnp.floor(total * jnp.exp2(15.0 - power) + 0.5)
        scaled = jnp.minimum(scaled, 32767.0)
        out_ref[i, :BS, :] = scaled.astype(jnp.int32).astype(jnp.int16)
        power = jnp.broadcast_to(power, (ROWS - BS, 128))
        out_ref[i, BS:, :] = power.astype(jnp.int32).astype(jnp.int16)


def unpack(in_ref, out_ref):
    def step(j, total):
        value = in_ref[j].astype(jnp.int32).astype(F32)
        return total + value[:BS] * jnp.exp2(value[BS : BS + 1] - 15.0)

    out_ref[...] = lax.fori_loop(0, in_ref.shape[0], step, jnp.zeros((BS, 128), F32), unroll=4)


def packed_sum(a, b):
    return pl.pallas_call(
        pack,
        out_shape=jax.ShapeDtypeStruct((64, ROWS, 128), jnp.int16),
        in_specs=[VMEM, VMEM],
        out_specs=VMEM,
        compiler_params=pltpu.CompilerParams(vmem_limit_bytes=8 << 20),
        name="pack",
    )(a, b)


def unpacked_sum(mixed):
    return pl.pallas_call(
        unpack,
        out_shape=jax.ShapeDtypeStruct((BS, 128), F32),
        in_specs=[VMEM],
        out_specs=VMEM,
        compiler_params=pltpu.CompilerParams(vmem_limit_bytes=4 << 20),
        name="unpack",
    )(mixed)


def shards(a_vals, a_cols, p_vals, p_cols):
    a = in_hbm(a_vals[:, 0])
    piece = run_stamp(p_cols, p_vals)
    hi, lo, turned, beside = fetch_and_multiply(piece, a_cols[:, 0].T, a)
    turned, other = run_other_half(hi, lo, beside, turned)
    met = send(other, OTHER_CORE)
    own = run_own_half(hi, lo, turned)
    packed = packed_sum(own, met)
    mixed = lax.all_to_all(packed, ("x", "yh", "z", "yl"), 0, 0, tiled=True)
    return unpacked_sum(mixed)


def solution(mesh):
    fine = Mesh(mesh.devices.reshape(SIZES), AXES)
    row, col = ("x", "yh", "core"), ("z", "yl")
    in_specs = (
        P(row, col, None, None),
        P(row, col, None),
        P(row + col, None, None),
        P(row + col, None),
    )
    return jax.shard_map(
        shards, mesh=fine, in_specs=in_specs, out_specs=P(row, col), check_vma=False
    )
```

```python
import functools

import jax
import jax.numpy as jnp
from jax import lax
from jax.experimental import pallas as pl
from jax.experimental.pallas import tpu as pltpu
from jax.sharding import Mesh
from jax.sharding import PartitionSpec as P


AXES = ("x", "yh", "core", "z", "yl")
SIZES = (4, 2, 2, 4, 2)
BF16 = jnp.bfloat16
F32 = jnp.float32
BS = 64
ROWS = 72
HALF_ROWS = 136


def linear(place):
    index = 0
    for at, size in zip(place, SIZES):
        index = index * size + at
    return index


def route(target):
    pairs = []
    for x in range(4):
        for yh in range(2):
            for core in range(2):
                for z in range(4):
                    for yl in range(2):
                        to_x, to_y, to_core, to_z = target(x, 2 * yh + yl, core, z)
                        to_x, to_y, to_z = to_x % 4, to_y % 4, to_z % 4
                        to = linear((to_x, to_y // 2, to_core, to_z, to_y % 2))
                        pairs.append((linear((x, yh, core, z, yl)), to))
    return pairs


def swap_y(y):
    return (y % 2) * 2 + y // 2


REFLECT = route(lambda x, y, c, z: (2 * x - z + 2, swap_y(y), c, x))
ACROSS_Y = route(lambda x, y, c, z: (x, y + 2, c, z))
OTHER_CORE = route(lambda x, y, c, z: (x, y, 1 - c, z))
NEXT_X = route(lambda x, y, c, z: (x + 1, y, c, z))
LAST_X = route(lambda x, y, c, z: (x - 1, y, c, z))
NEXT_Z = route(lambda x, y, c, z: (x, y, c, z + 1))
LAST_Z = route(lambda x, y, c, z: (x, y, c, z - 1))
ACROSS_Z = route(lambda x, y, c, z: (x, y, c, z + 2))
BESIDE = route(lambda x, y, c, z: (x, y ^ 1, c, z))


def send(value, pairs):
    return lax.ppermute(value, AXES, pairs)


def together(*values):
    return lax.optimization_barrier(values)


def rows16(row):
    return jnp.broadcast_to(row.astype(F32), (16, 128)).astype(BF16)


def choose(ids, number, values):
    out = [jnp.zeros((16, 128), BF16)] * 4
    for value, at in zip(values, ids):
        hit = at == number
        out = [jnp.where(hit, value[16 * t : 16 * (t + 1)], out[t]) for t in range(4)]
    return jnp.concatenate(out, axis=0)


def swap_halves(v):
    return jnp.concatenate([v[:, BS:], v[:, :BS]], axis=1)


def meet(first, free, last):
    fixed = together(*first, *last)
    return fixed[: len(first)] + free + fixed[len(first) :]


def spread(tile, ids, store):
    low = lax.broadcasted_iota(jnp.int32, (BS, 128), 1) < BS
    low1 = lax.broadcasted_iota(jnp.int32, (1, 128), 1) < BS
    values, where = [], []
    for pair in range(2):
        v = tile[:, 128 * pair : 128 * (pair + 1)].astype(F32)
        r = swap_halves(v)
        d = ids[:, 128 * pair : 128 * (pair + 1)]
        e = swap_halves(d)
        values += [jnp.where(low, v, r).astype(BF16), jnp.where(low, r, v).astype(BF16)]
        for full in (jnp.where(low1, d, e), jnp.where(low1, e, d)):
            where.append(rows16(full - jnp.where(low1, 0.0, 1.0)))
    for g in range(8):
        store(g, choose(where, jnp.asarray(2.0 * g, BF16), values))


def position(name):
    return lax.axis_index(name).astype(jnp.int32)


def flip(bit, number):
    return bit if number == 0 else 1 - bit


NEAR = ((0, 0, 0, 2),)
BEHIND, AHEAD, ACROSS = ((-1, 0, 0, 2),), ((1, 0, 0, 2),), ((0, 1, 0, 2),)
BEHIND2, AHEAD2 = ((-1, 1, 0, 2), (2, 0, 0, 1)), ((1, 1, 0, 2), (2, 0, 1, 1))
BEHIND3, AHEAD3 = ((2, 1, 0, 1),), ((2, 1, 1, 1),)


def place(ref, halves, other, dense):
    x, yh, core, z = (position(name) for name in ("x", "yh", "core", "z"))
    owner = 1 - core if other else core
    base = 0
    for step, side, first, count in halves:
        piece = 2 * jnp.bitwise_and(2 * z + 10 - x - step, 3) + flip(yh, side)
        at = 32 * owner + 4 * piece + 2 * first

        def one(h, base=base, at=at):
            ids = ref[base + h, pl.ds(2 * BS, 8), :].astype(F32)
            for b in range(2):

                def store(g, out):
                    dense[at + 2 * h + b, :, 128 * g : 128 * (g + 1)] = out

                spread(ref[base + h, pl.ds(BS * b, BS), :], ids[b : b + 1], store)

        if count == 1:
            one(0)
        else:
            pl.loop(0, count)(one)
        base += count


def place_all(what, *refs):
    for (halves, other), ref in zip(what, refs):
        place(ref, halves, other, refs[-1])


def fine_product(what, cols_ref, a_ref, *refs):
    arrays, (dense_in, hi, lo, dense) = refs[: len(what)], refs[len(what) :]
    place_all(what, *arrays, dense)

    @pl.loop(0, a_ref.shape[0])
    def _(i):
        for n in range(4):
            total = None
            for k in range(4):
                tiles = [
                    dense[cols_ref[4 * k + j, i], :, 256 * n : 256 * (n + 1)] for j in range(4)
                ]
                weights = jnp.concatenate(tiles, axis=0)
                left = a_ref[i, :, 256 * k : 256 * (k + 1)]
                part = jnp.dot(left, weights, preferred_element_type=F32)
                total = part if total is None else total + part
            top = total.astype(BF16)
            rows = pl.ds(pl.multiple_of(i * BS, BS), BS)
            hi[rows, 256 * n : 256 * (n + 1)] = top
            lo[rows, 256 * n : 256 * (n + 1)] = (total - top.astype(F32)).astype(BF16)


def turn(ref, h, turned, core, at):
    ids = ref[h, pl.ds(2 * BS, 8), :].astype(F32)
    flipped = ref[h, pl.ds(0, 128), :].astype(F32).T.astype(BF16)
    where, values = [], []
    for m in range(4):
        a = ids[0:1, BS * m : BS * (m + 1)]
        b = ids[1:2, BS * m : BS * (m + 1)]
        where.append(rows16(jnp.concatenate([a, b], axis=1)))
        values.append(flipped[BS * m : BS * (m + 1)])
    for n in range(16):
        out = choose(where, jnp.asarray(float(n), BF16), values)
        slot = core if n % 2 == 0 else 1 - core
        turned[slot, pl.ds(BS * (n // 2), BS), pl.ds(pl.multiple_of(at, 128), 128)] = out


def half_product(turned, slot, hi, lo, out_ref):
    @pl.loop(0, 4)
    def _(n):
        at = pl.ds(pl.multiple_of(256 * n, 256), 256)
        left = jnp.concatenate([turned[slot], turned[slot]], axis=1)
        c = jnp.dot(left, jnp.concatenate([hi[:, at], lo[:, at]]), preferred_element_type=F32)
        store_blocks(c, n, out_ref)


def turn_line(ref, side, turned):
    core, z, yl = (position(name) for name in ("core", "z", "yl"))
    for ring, step in enumerate((0, -1, 1, 2)):
        at = 256 * (2 * jnp.bitwise_and(z + step + 4, 3) + flip(yl, side))

        @pl.loop(0, 2)
        def _(h):
            turn(ref, 2 * ring + h, turned, core, at + 128 * h)


def turn_own(line, turned):
    turn_line(line, 0, turned)


def store_blocks(c, n, out_ref):
    for q in range(8):
        for j in range(2):
            out_ref[16 * (q // 2) + 4 * n + 2 * (q % 2) + j] = c[BS * q : BS * (q + 1), 128 * j : 128 * (j + 1)]


def other_half(hi, lo, beside, turned_in, turned, out_ref):
    turn_line(beside, 1, turned)
    half_product(turned, 1, hi, lo, out_ref)


def own_half(hi, lo, turned, out_ref):
    half_product(turned, 0, hi, lo, out_ref)


def in_hbm(v):
    return pltpu.with_memory_space_constraint(v, pltpu.HBM)


VMEM = pl.BlockSpec(memory_space=pltpu.VMEM)
SMEM = pl.BlockSpec(memory_space=pltpu.SMEM)
HBM = pl.BlockSpec(memory_space=pltpu.HBM)
HALF = jax.ShapeDtypeStruct((64, BS, 128), F32)


def cost(flops):
    return pl.CostEstimate(flops=flops, bytes_accessed=1 << 23, transcendentals=0)


DENSE = pltpu.VMEM((64, BS, 1024), BF16)


def run_place(what, arrays, dense, a=None):
    given = () if dense is None else (dense,)
    fetched = () if a is None else (a,)
    count = len(arrays) + len(given)

    def body(*refs):
        if a is None:
            place_all(what, *refs[: len(what)], refs[-1])
        else:
            fetch = pltpu.make_async_copy(refs[count], refs[count + 2], refs[-1])
            fetch.start()
            place_all(what, *refs[: len(what)], refs[count + 1])
            fetch.wait()

    call = pl.pallas_call(
        body,
        out_shape=(DENSE,) + tuple(pltpu.VMEM(v.shape, v.dtype) for v in fetched),
        in_specs=[VMEM] * count + [HBM] * len(fetched),
        out_specs=(VMEM,) * (1 + len(fetched)),
        scratch_shapes=[pltpu.SemaphoreType.DMA] * len(fetched),
        input_output_aliases={len(arrays): 0} if given else {},
        compiler_params=pltpu.CompilerParams(vmem_limit_bytes=16 << 20),
        cost_estimate=cost(1 << 30),
    )
    out = call(*arrays, *given, *fetched)
    return out if fetched else out[0]


def run_fine_product(what, cols, a, arrays, dense):
    rows = a.shape[0] * BS
    return pl.pallas_call(
        functools.partial(fine_product, what),
        out_shape=(pltpu.VMEM((rows, 1024), BF16),) * 2 + (DENSE,),
        in_specs=[SMEM] + [VMEM] * (len(arrays) + 2),
        out_specs=(VMEM,) * 3,
        input_output_aliases={2 + len(arrays): 2},
        compiler_params=pltpu.CompilerParams(vmem_limit_bytes=16 << 20),
        cost_estimate=cost(2 << 33),
        name="fine_product",
    )(cols, a, *arrays, dense)


def run_turn(line):
    return pl.pallas_call(
        turn_own,
        out_shape=pltpu.VMEM((2, 512, 2048), BF16),
        in_specs=[VMEM],
        out_specs=VMEM,
        compiler_params=pltpu.CompilerParams(vmem_limit_bytes=8 << 20),
        cost_estimate=cost(1 << 30),
        name="turn",
    )(line)


def run_other_half(hi, lo, beside, turned):
    return pl.pallas_call(
        other_half,
        out_shape=(pltpu.VMEM(turned.shape, BF16), HALF),
        in_specs=[VMEM] * 4,
        out_specs=(VMEM, VMEM),
        input_output_aliases={3: 0},
        compiler_params=pltpu.CompilerParams(vmem_limit_bytes=20 << 20),
        cost_estimate=cost(1 << 33),
        name="other_half",
    )(hi, lo, beside, turned)


def run_own_half(hi, lo, turned):
    return pl.pallas_call(
        own_half,
        out_shape=HALF,
        in_specs=[VMEM] * 3,
        out_specs=VMEM,
        compiler_params=pltpu.CompilerParams(vmem_limit_bytes=16 << 20),
        cost_estimate=cost(1 << 33),
        name="own_half",
    )(hi, lo, turned)


def stamp(cols_ref, vals_ref, out_ref, sems):
    copies = []
    for b in range(4):
        to = out_ref.at[b // 2, pl.ds(BS * (b % 2), BS)]
        copies.append(pltpu.make_async_copy(vals_ref.at[b], to, sems.at[b]))
        copies[b].start()
    block = lax.broadcasted_iota(jnp.int32, (1, 4 * BS), 1) // BS
    for h in range(2):
        rows = []
        for b in range(2):
            row = jnp.zeros((1, 4 * BS), jnp.int32)
            for m in range(4):
                row = jnp.where(block == m, cols_ref[2 * h + b, m], row)
            rows.append(row)
        rows.append(jnp.zeros((6, 4 * BS), jnp.int32))
        out_ref[h, 2 * BS :, :] = jnp.concatenate(rows).astype(F32).astype(BF16)
    for copy in copies:
        copy.wait()


def run_stamp(cols, vals):
    return pl.pallas_call(
        stamp,
        out_shape=jax.ShapeDtypeStruct((2, HALF_ROWS, 4 * BS), BF16),
        in_specs=[SMEM, HBM],
        out_specs=VMEM,
        scratch_shapes=[pltpu.SemaphoreType.DMA((4,))],
        compiler_params=pltpu.CompilerParams(vmem_limit_bytes=2 << 20),
        name="stamp",
    )(in_hbm(cols), in_hbm(vals))


def fetch_and_multiply(piece, cols, a):
    (near,) = together(send(piece, REFLECT))
    b1, a1, f, z1, z2, z3, dense = meet(
        (send(near, NEXT_X), send(near, LAST_X), send(near, ACROSS_Y)),
        (send(piece, NEXT_Z), send(piece, LAST_Z), send(piece, ACROSS_Z)),
        (run_place(((NEAR, False),), (near,), None),),
    )
    what = ((BEHIND, False), (AHEAD, False), (ACROSS, False))
    line = jnp.concatenate([piece, z1, z2, z3])
    b2, a2, e1, line, dense, turned = together(
        send(jnp.concatenate([f, b1[:1]]), NEXT_X),
        send(jnp.concatenate([f, a1[1:]]), LAST_X),
        send(jnp.concatenate([near, b1, a1, f]), OTHER_CORE),
        line,
        run_place(what, (b1, a1, f), dense),
        run_turn(line),
    )
    what = ((BEHIND2, False), (AHEAD2, False), (NEAR + BEHIND + AHEAD + ACROSS, True))
    beside = send(line, BESIDE)
    b3, a3, e2, (dense, a) = together(
        send(b2[:1], NEXT_X),
        send(a2[1:2], LAST_X),
        send(jnp.concatenate([b2, a2]), OTHER_CORE),
        run_place(what, (b2, a2, e1), dense, a),
    )
    e3 = send(jnp.concatenate([b3, a3]), OTHER_CORE)
    what = ((BEHIND3, False), (AHEAD3, False), (BEHIND2 + AHEAD2, True))
    dense = run_place(what, (b3, a3, e2), dense)
    what = ((BEHIND3 + AHEAD3, True),)
    hi, lo, dense = run_fine_product(what, cols, a, (e3,), dense)
    return hi, lo, turned, beside


def pack(a_ref, b_ref, out_ref):
    @pl.loop(0, a_ref.shape[0] // 4)
    def _(four):
        for i in range(4):
            at = 4 * four + i
            total = a_ref[at] + b_ref[at]
            largest = jnp.max(jnp.abs(total), axis=0, keepdims=True)
            power = jnp.clip(jnp.ceil(jnp.log2(jnp.maximum(largest, 1e-36))), -110.0, 60.0)
            scaled = jnp.floor(total * jnp.exp2(15.0 - power) + 0.5)
            scaled = jnp.minimum(scaled, 32767.0)
            out_ref[at, :BS, :] = scaled.astype(jnp.int32).astype(jnp.int16)
            power = jnp.broadcast_to(power, (ROWS - BS, 128))
            out_ref[at, BS:, :] = power.astype(jnp.int32).astype(jnp.int16)


def unpack(in_ref, out_ref):
    def step(j, total):
        value = in_ref[j].astype(jnp.int32).astype(F32)
        return total + value[:BS] * jnp.exp2(value[BS : BS + 1] - 15.0)

    out_ref[...] = lax.fori_loop(0, in_ref.shape[0], step, jnp.zeros((BS, 128), F32), unroll=4)


def packed_sum(a, b):
    return pl.pallas_call(
        pack,
        out_shape=jax.ShapeDtypeStruct((64, ROWS, 128), jnp.int16),
        in_specs=[VMEM, VMEM],
        out_specs=VMEM,
        compiler_params=pltpu.CompilerParams(vmem_limit_bytes=8 << 20),
        name="pack",
    )(a, b)


def unpacked_sum(mixed):
    return pl.pallas_call(
        unpack,
        out_shape=jax.ShapeDtypeStruct((BS, 128), F32),
        in_specs=[VMEM],
        out_specs=VMEM,
        compiler_params=pltpu.CompilerParams(vmem_limit_bytes=4 << 20),
        name="unpack",
    )(mixed)


def shards(a_vals, a_cols, p_vals, p_cols):
    a = in_hbm(a_vals[:, 0])
    piece = run_stamp(p_cols, p_vals)
    hi, lo, turned, beside = fetch_and_multiply(piece, a_cols[:, 0].T, a)
    turned, other = run_other_half(hi, lo, beside, turned)
    met = send(other, OTHER_CORE)
    own = run_own_half(hi, lo, turned)
    packed = packed_sum(own, met)
    mixed = lax.all_to_all(packed, ("x", "z", "yh", "yl"), 0, 0, tiled=True)
    return unpacked_sum(mixed)


def solution(mesh):
    fine = Mesh(mesh.devices.reshape(SIZES), AXES)
    row, col = ("x", "yh", "core"), ("z", "yl")
    in_specs = (
        P(row, col, None, None),
        P(row, col, None),
        P(row + col, None, None),
        P(row + col, None),
    )
    return jax.shard_map(
        shards, mesh=fine, in_specs=in_specs, out_specs=P(row, col), check_vma=False
    )
```

```python
import functools

import jax
import jax.numpy as jnp
from jax import lax
from jax.experimental import pallas as pl
from jax.experimental.pallas import tpu as pltpu
from jax.sharding import Mesh
from jax.sharding import PartitionSpec as P


AXES = ("x", "yh", "core", "z", "yl")
SIZES = (4, 2, 2, 4, 2)
BF16 = jnp.bfloat16
F32 = jnp.float32
BS = 64
ROWS = 72
HALF_ROWS = 136


def linear(place):
    index = 0
    for at, size in zip(place, SIZES):
        index = index * size + at
    return index


def route(target):
    pairs = []
    for x in range(4):
        for yh in range(2):
            for core in range(2):
                for z in range(4):
                    for yl in range(2):
                        to_x, to_y, to_core, to_z = target(x, 2 * yh + yl, core, z)
                        to_x, to_y, to_z = to_x % 4, to_y % 4, to_z % 4
                        to = linear((to_x, to_y // 2, to_core, to_z, to_y % 2))
                        pairs.append((linear((x, yh, core, z, yl)), to))
    return pairs


def swap_y(y):
    return (y % 2) * 2 + y // 2


REFLECT = route(lambda x, y, c, z: (2 * x - z + 2, swap_y(y), c, x))
ACROSS_Y = route(lambda x, y, c, z: (x, y + 2, c, z))
OTHER_CORE = route(lambda x, y, c, z: (x, y, 1 - c, z))
NEXT_X = route(lambda x, y, c, z: (x + 1, y, c, z))
LAST_X = route(lambda x, y, c, z: (x - 1, y, c, z))
NEXT_Z = route(lambda x, y, c, z: (x, y, c, z + 1))
LAST_Z = route(lambda x, y, c, z: (x, y, c, z - 1))
ACROSS_Z = route(lambda x, y, c, z: (x, y, c, z + 2))
BESIDE = route(lambda x, y, c, z: (x, y ^ 1, c, z))


def send(value, pairs):
    return lax.ppermute(value, AXES, pairs)


def together(*values):
    return lax.optimization_barrier(values)


def rows16(row):
    return jnp.broadcast_to(row.astype(F32), (16, 128)).astype(BF16)


def choose(ids, number, values):
    out = [jnp.zeros((16, 128), BF16)] * 4
    for value, at in zip(values, ids):
        hit = at == number
        out = [jnp.where(hit, value[16 * t : 16 * (t + 1)], out[t]) for t in range(4)]
    return jnp.concatenate(out, axis=0)


def swap_halves(v):
    return jnp.concatenate([v[:, BS:], v[:, :BS]], axis=1)


def meet(first, free, last):
    fixed = together(*first, *last)
    return fixed[: len(first)] + free + fixed[len(first) :]


def spread(tile, ids, store):
    low = lax.broadcasted_iota(jnp.int32, (BS, 128), 1) < BS
    low1 = lax.broadcasted_iota(jnp.int32, (1, 128), 1) < BS
    values, where = [], []
    for pair in range(2):
        v = tile[:, 128 * pair : 128 * (pair + 1)].astype(F32)
        r = swap_halves(v)
        d = ids[:, 128 * pair : 128 * (pair + 1)]
        e = swap_halves(d)
        values += [jnp.where(low, v, r).astype(BF16), jnp.where(low, r, v).astype(BF16)]
        for full in (jnp.where(low1, d, e), jnp.where(low1, e, d)):
            where.append(rows16(full - jnp.where(low1, 0.0, 1.0)))
    for g in range(8):
        store(g, choose(where, jnp.asarray(2.0 * g, BF16), values))


def position(name):
    return lax.axis_index(name).astype(jnp.int32)


def flip(bit, number):
    return bit if number == 0 else 1 - bit


NEAR = ((0, 0, 0, 2),)
BEHIND, AHEAD, ACROSS = ((-1, 0, 0, 2),), ((1, 0, 0, 2),), ((0, 1, 0, 2),)
BEHIND2, AHEAD2 = ((-1, 1, 0, 2), (2, 0, 0, 1)), ((1, 1, 0, 2), (2, 0, 1, 1))
BEHIND3, AHEAD3 = ((2, 1, 0, 1),), ((2, 1, 1, 1),)


def place(ref, halves, other, dense):
    x, yh, core, z = (position(name) for name in ("x", "yh", "core", "z"))
    owner = 1 - core if other else core
    base = 0
    for step, side, first, count in halves:
        piece = 2 * jnp.bitwise_and(2 * z + 10 - x - step, 3) + flip(yh, side)
        at = 32 * owner + 4 * piece + 2 * first

        def one(h, base=base, at=at):
            ids = ref[base + h, pl.ds(2 * BS, 8), :].astype(F32)
            for b in range(2):

                def store(g, out):
                    dense[at + 2 * h + b, :, 128 * g : 128 * (g + 1)] = out

                spread(ref[base + h, pl.ds(BS * b, BS), :], ids[b : b + 1], store)

        if count == 1:
            one(0)
        else:
            pl.loop(0, count)(one)
        base += count


def place_all(what, *refs):
    for (halves, other), ref in zip(what, refs):
        place(ref, halves, other, refs[-1])


def fine_product(what, cols_ref, a_ref, *refs):
    arrays, (dense_in, hi, lo, dense) = refs[: len(what)], refs[len(what) :]
    place_all(what, *arrays, dense)

    @pl.loop(0, a_ref.shape[0])
    def _(i):
        for n in range(4):
            total = None
            for k in range(4):
                tiles = [
                    dense[cols_ref[4 * k + j, i], :, 256 * n : 256 * (n + 1)] for j in range(4)
                ]
                weights = jnp.concatenate(tiles, axis=0)
                left = a_ref[i, :, 256 * k : 256 * (k + 1)]
                part = jnp.dot(left, weights, preferred_element_type=F32)
                total = part if total is None else total + part
            top = total.astype(BF16)
            rows = pl.ds(pl.multiple_of(i * BS, BS), BS)
            hi[rows, 256 * n : 256 * (n + 1)] = top
            lo[rows, 256 * n : 256 * (n + 1)] = (total - top.astype(F32)).astype(BF16)


def turn(ref, h, turned, core, at):
    ids = ref[h, pl.ds(2 * BS, 8), :].astype(F32)
    flipped = ref[h, pl.ds(0, 128), :].astype(F32).T.astype(BF16)
    where, values = [], []
    for m in range(4):
        a = ids[0:1, BS * m : BS * (m + 1)]
        b = ids[1:2, BS * m : BS * (m + 1)]
        where.append(rows16(jnp.concatenate([a, b], axis=1)))
        values.append(flipped[BS * m : BS * (m + 1)])
    for n in range(16):
        out = choose(where, jnp.asarray(float(n), BF16), values)
        slot = core if n % 2 == 0 else 1 - core
        turned[slot, pl.ds(BS * (n // 2), BS), pl.ds(pl.multiple_of(at, 128), 128)] = out


def half_product(turned, slot, hi, lo, out_ref):
    @pl.loop(0, 4)
    def _(n):
        at = pl.ds(pl.multiple_of(256 * n, 256), 256)
        left = jnp.concatenate([turned[slot], turned[slot]], axis=1)
        c = jnp.dot(left, jnp.concatenate([hi[:, at], lo[:, at]]), preferred_element_type=F32)
        store_blocks(c, n, out_ref)


def turn_line(ref, side, turned):
    core, z, yl = (position(name) for name in ("core", "z", "yl"))
    for ring, step in enumerate((0, -1, 1, 2)):
        at = 256 * (2 * jnp.bitwise_and(z + step + 4, 3) + flip(yl, side))

        @pl.loop(0, 2)
        def _(h):
            turn(ref, 2 * ring + h, turned, core, at + 128 * h)


def turn_own(line, turned):
    turn_line(line, 0, turned)


def store_blocks(c, n, out_ref):
    for q in range(8):
        for j in range(2):
            out_ref[16 * (q // 2) + 4 * n + 2 * (q % 2) + j] = c[BS * q : BS * (q + 1), 128 * j : 128 * (j + 1)]


def other_half(hi, lo, beside, turned_in, turned, out_ref):
    turn_line(beside, 1, turned)
    half_product(turned, 1, hi, lo, out_ref)


def own_half(hi, lo, turned, out_ref):
    half_product(turned, 0, hi, lo, out_ref)


def in_hbm(v):
    return pltpu.with_memory_space_constraint(v, pltpu.HBM)


VMEM = pl.BlockSpec(memory_space=pltpu.VMEM)
SMEM = pl.BlockSpec(memory_space=pltpu.SMEM)
HBM = pl.BlockSpec(memory_space=pltpu.HBM)
HALF = jax.ShapeDtypeStruct((64, BS, 128), F32)


def cost(flops):
    return pl.CostEstimate(flops=flops, bytes_accessed=1 << 23, transcendentals=0)


DENSE = pltpu.VMEM((64, BS, 1024), BF16)


def run_place(what, arrays, dense, a=None):
    given = () if dense is None else (dense,)
    fetched = () if a is None else (a,)
    count = len(arrays) + len(given)

    def body(*refs):
        if a is None:
            place_all(what, *refs[: len(what)], refs[-1])
        else:
            fetch = pltpu.make_async_copy(refs[count], refs[count + 2], refs[-1])
            fetch.start()
            place_all(what, *refs[: len(what)], refs[count + 1])
            fetch.wait()

    call = pl.pallas_call(
        body,
        out_shape=(DENSE,) + tuple(pltpu.VMEM(v.shape, v.dtype) for v in fetched),
        in_specs=[VMEM] * count + [HBM] * len(fetched),
        out_specs=(VMEM,) * (1 + len(fetched)),
        scratch_shapes=[pltpu.SemaphoreType.DMA] * len(fetched),
        input_output_aliases={len(arrays): 0} if given else {},
        compiler_params=pltpu.CompilerParams(vmem_limit_bytes=16 << 20),
        cost_estimate=cost(1 << 30),
    )
    out = call(*arrays, *given, *fetched)
    return out if fetched else out[0]


def run_fine_product(what, cols, a, arrays, dense):
    rows = a.shape[0] * BS
    return pl.pallas_call(
        functools.partial(fine_product, what),
        out_shape=(pltpu.VMEM((rows, 1024), BF16),) * 2 + (DENSE,),
        in_specs=[SMEM] + [VMEM] * (len(arrays) + 2),
        out_specs=(VMEM,) * 3,
        input_output_aliases={2 + len(arrays): 2},
        compiler_params=pltpu.CompilerParams(vmem_limit_bytes=16 << 20),
        cost_estimate=cost(2 << 33),
        name="fine_product",
    )(cols, a, *arrays, dense)


def run_turn(line):
    return pl.pallas_call(
        turn_own,
        out_shape=pltpu.VMEM((2, 512, 2048), BF16),
        in_specs=[VMEM],
        out_specs=VMEM,
        compiler_params=pltpu.CompilerParams(vmem_limit_bytes=8 << 20),
        cost_estimate=cost(1 << 30),
        name="turn",
    )(line)


def run_other_half(hi, lo, beside, turned):
    return pl.pallas_call(
        other_half,
        out_shape=(pltpu.VMEM(turned.shape, BF16), HALF),
        in_specs=[VMEM] * 4,
        out_specs=(VMEM, VMEM),
        input_output_aliases={3: 0},
        compiler_params=pltpu.CompilerParams(vmem_limit_bytes=20 << 20),
        cost_estimate=cost(1 << 33),
        name="other_half",
    )(hi, lo, beside, turned)


def run_own_half(hi, lo, turned):
    return pl.pallas_call(
        own_half,
        out_shape=HALF,
        in_specs=[VMEM] * 3,
        out_specs=VMEM,
        compiler_params=pltpu.CompilerParams(vmem_limit_bytes=16 << 20),
        cost_estimate=cost(1 << 33),
        name="own_half",
    )(hi, lo, turned)


def stamp(cols_ref, vals_ref, out_ref, sems):
    copies = []
    for b in range(4):
        to = out_ref.at[b // 2, pl.ds(BS * (b % 2), BS)]
        copies.append(pltpu.make_async_copy(vals_ref.at[b], to, sems.at[b]))
        copies[b].start()
    block = lax.broadcasted_iota(jnp.int32, (1, 4 * BS), 1) // BS
    for h in range(2):
        rows = []
        for b in range(2):
            row = jnp.zeros((1, 4 * BS), jnp.int32)
            for m in range(4):
                row = jnp.where(block == m, cols_ref[2 * h + b, m], row)
            rows.append(row)
        rows.append(jnp.zeros((6, 4 * BS), jnp.int32))
        out_ref[h, 2 * BS :, :] = jnp.concatenate(rows).astype(F32).astype(BF16)
    for copy in copies:
        copy.wait()


def run_stamp(cols, vals):
    return pl.pallas_call(
        stamp,
        out_shape=jax.ShapeDtypeStruct((2, HALF_ROWS, 4 * BS), BF16),
        in_specs=[SMEM, HBM],
        out_specs=VMEM,
        scratch_shapes=[pltpu.SemaphoreType.DMA((4,))],
        compiler_params=pltpu.CompilerParams(vmem_limit_bytes=2 << 20),
        name="stamp",
    )(in_hbm(cols), in_hbm(vals))


def fetch_and_multiply(piece, cols, a):
    (near,) = together(send(piece, REFLECT))
    b1, a1, f, z1, z2, z3, dense = meet(
        (send(near, NEXT_X), send(near, LAST_X), send(near, ACROSS_Y)),
        (send(piece, NEXT_Z), send(piece, LAST_Z), send(piece, ACROSS_Z)),
        (run_place(((NEAR, False),), (near,), None),),
    )
    what = ((BEHIND, False), (AHEAD, False), (ACROSS, False))
    line = jnp.concatenate([piece, z1, z2, z3])
    turned = run_turn(line)
    beside = send(line, BESIDE)
    b2, a2, e1, dense = together(
        send(jnp.concatenate([f, b1[:1]]), NEXT_X),
        send(jnp.concatenate([f, a1[1:]]), LAST_X),
        send(jnp.concatenate([near, b1, a1, f]), OTHER_CORE),
        run_place(what, (b1, a1, f), dense),
    )
    what = ((BEHIND2, False), (AHEAD2, False), (NEAR + BEHIND + AHEAD + ACROSS, True))
    b3, a3, e2, (dense, a) = together(
        send(b2[:1], NEXT_X),
        send(a2[1:2], LAST_X),
        send(jnp.concatenate([b2, a2]), OTHER_CORE),
        run_place(what, (b2, a2, e1), dense, a),
    )
    e3 = send(jnp.concatenate([b3, a3]), OTHER_CORE)
    what = ((BEHIND3, False), (AHEAD3, False), (BEHIND2 + AHEAD2, True))
    dense = run_place(what, (b3, a3, e2), dense)
    what = ((BEHIND3 + AHEAD3, True),)
    hi, lo, dense = run_fine_product(what, cols, a, (e3,), dense)
    return hi, lo, turned, beside


def pack(a_ref, b_ref, out_ref):
    @pl.loop(0, a_ref.shape[0] // 4)
    def _(four):
        for i in range(4):
            at = 4 * four + i
            total = a_ref[at] + b_ref[at]
            largest = jnp.max(jnp.abs(total), axis=0, keepdims=True)
            power = jnp.clip(jnp.ceil(jnp.log2(jnp.maximum(largest, 1e-36))), -110.0, 60.0)
            scaled = jnp.floor(total * jnp.exp2(15.0 - power) + 0.5)
            scaled = jnp.minimum(scaled, 32767.0)
            out_ref[at, :BS, :] = scaled.astype(jnp.int32).astype(jnp.int16)
            power = jnp.broadcast_to(power, (ROWS - BS, 128))
            out_ref[at, BS:, :] = power.astype(jnp.int32).astype(jnp.int16)


def unpack(in_ref, out_ref):
    def step(j, total):
        value = in_ref[j].astype(jnp.int32).astype(F32)
        return total + value[:BS] * jnp.exp2(value[BS : BS + 1] - 15.0)

    out_ref[...] = lax.fori_loop(0, in_ref.shape[0], step, jnp.zeros((BS, 128), F32), unroll=4)


def packed_sum(a, b):
    return pl.pallas_call(
        pack,
        out_shape=jax.ShapeDtypeStruct((64, ROWS, 128), jnp.int16),
        in_specs=[VMEM, VMEM],
        out_specs=VMEM,
        compiler_params=pltpu.CompilerParams(vmem_limit_bytes=8 << 20),
        name="pack",
    )(a, b)


def unpacked_sum(mixed):
    return pl.pallas_call(
        unpack,
        out_shape=jax.ShapeDtypeStruct((BS, 128), F32),
        in_specs=[VMEM],
        out_specs=VMEM,
        compiler_params=pltpu.CompilerParams(vmem_limit_bytes=4 << 20),
        name="unpack",
    )(mixed)


def shards(a_vals, a_cols, p_vals, p_cols):
    a = in_hbm(a_vals[:, 0])
    piece = run_stamp(p_cols, p_vals)
    hi, lo, turned, beside = fetch_and_multiply(piece, a_cols[:, 0].T, a)
    turned, other = run_other_half(hi, lo, beside, turned)
    met = send(other, OTHER_CORE)
    own = run_own_half(hi, lo, turned)
    packed = packed_sum(own, met)
    mixed = lax.all_to_all(packed, ("x", "z", "yh", "yl"), 0, 0, tiled=True)
    return unpacked_sum(mixed)


def solution(mesh):
    fine = Mesh(mesh.devices.reshape(SIZES), AXES)
    row, col = ("x", "yh", "core"), ("z", "yl")
    in_specs = (
        P(row, col, None, None),
        P(row, col, None),
        P(row + col, None, None),
        P(row + col, None),
    )
    return jax.shard_map(
        shards, mesh=fine, in_specs=in_specs, out_specs=P(row, col), check_vma=False
    )
```
